32 devices in a mesh: lon: 8 (over z, x), lat: 4 (over y, core).
Axes of the slice: x: 2, y: 2, z: 4, core: 2. Of those that a mesh axis runs over, the one named last changes fastest.
Arguments:
- expanded: bfloat16 [32, 128, 3072], P('lat', 'lon'), may hold values from -6 to 6
- stream: bfloat16 [32, 128, 768], P('lat', 'lon'), may hold values from -6 to 6
- land: int32 [32, 128], P('lat', 'lon'), may hold values 0 or 1
- polar: int32 [32], replicated, may hold values from 0 to 1, as said below
- land_shift: float32 [3072], replicated, may hold values from -4 to 4
- dw_kernel: float32 [3, 3, 3072], replicated, may hold values from -2 to 2
- w_proj: bfloat16 [3072, 768], replicated, may hold values from -0.109375 to 0.109375
- w_qkv: bfloat16 [768, 2304], replicated, may hold values from -0.21875 to 0.21875
- w_out: bfloat16 [768, 768], replicated, may hold values from -0.21875 to 0.21875
- rel_bias: float32 [24, 15, 8], replicated, may hold values from -2 to 250
Outputs:
- mixed_out: bfloat16 [32, 128, 768], P('lat', 'lon')
The draws below stay inside these ranges and needn't reach their ends.
Inputs may be any that keep to these rules, and one draw needn't show every extreme that they name: `polar`: 1 marks the first a and the last b token rows, 1 <= a, b <= 4, at least one of a, b equal to 4; all other rows are 0.
All inputs are finite; a program needn't handle non-finite values. No bound on the sum of `land` on one device may be relied on, other than what follows from the above.
Results may differ from the reference program's by a relative error of at most 0.0075.
Values may be sent and summed in bfloat16 or wider, within the bound.
A program may use at most 128 MiB of HBM per device.

```python
import jax
import jax.numpy as jnp
import numpy as np
from jax import lax

D = 768
HEADS = 24
EXP = 3072
GRID = 8
CAP = 4
ROWS = 32
COLS = 128


def draw_polar(key, part):
    first, second, third = jax.random.split(jax.random.fold_in(key, 11), 3)
    top = jax.random.randint(first, (), 1, CAP + 1)
    bottom = jax.random.randint(second, (), 1, CAP + 1)
    side = jax.random.randint(third, (), 0, 2)
    top = jnp.where(side == 0, CAP, top)
    bottom = jnp.where(side == 1, CAP, bottom)
    rows = jnp.arange(ROWS)
    return ((rows < top) | (rows >= ROWS - bottom)).astype(jnp.int32)


def draw_rel_bias(key, part):
    base_key = jax.random.fold_in(jax.random.fold_in(key, 23), 0)
    table = jax.random.uniform(base_key, (HEADS, 2 * GRID - 1, GRID), jnp.float32, -2.0, 2.0)
    return table.astype(jnp.float32)


def place_ends(drawn, rng, low, largest):
    index_at = [jax.random.randint(jax.random.fold_in(rng, axis), (), 0, length) for axis, length in enumerate(drawn.shape)]
    widest = drawn.shape.index(max(drawn.shape))
    neighbour = index_at[:widest] + [(index_at[widest] + 1) % drawn.shape[widest]] + index_at[widest + 1:]
    return drawn.at[tuple(index_at)].set(low).at[tuple(neighbour)].set(largest)


def steps_of(own_key, shape, cuts, low, largest):
    factor_of = 1.0
    for axis_at, shards_of in cuts:
        heights = jax.random.uniform(jax.random.fold_in(jax.random.fold_in(own_key, 6), axis_at), (shards_of,), jnp.float32, low / len(cuts), largest / len(cuts))
        factor_of = factor_of * jnp.repeat(jnp.exp(heights), shape[axis_at] // shards_of).reshape((-1,) + (1,) * (len(shape) - 1 - axis_at))
    return factor_of


def scatter_about(rng, dims, scale, bound, cuts=(), held_as=jnp.bfloat16):
    values = scale * jax.random.normal(rng, dims, jnp.float32)
    if cuts:
        values = values * steps_of(rng, dims, cuts, -0.22, 0.18)
    return jnp.clip(values, -bound, bound).astype(held_as)


def setup_inputs(seed: int = 0) -> dict:
    key_of = jax.random.split(jax.random.key(seed), 11)
    expanded = scatter_about(key_of[0], (ROWS, COLS, EXP), 1.0, 6.0, ((0, 4), (1, 8)))
    stream = scatter_about(key_of[1], (ROWS, COLS, D), 1.0, 6.0, ((0, 4), (1, 8)))
    land = place_ends((jax.random.randint(key_of[2], (ROWS, COLS), 0, 10) < 3).astype(jnp.int32), jax.random.fold_in(key_of[2], 1), 0, 1)
    polar = draw_polar(jax.random.fold_in(key_of[10], 71), 0)
    land_shift = scatter_about(key_of[4], (EXP,), 1.0, 4.0, (), jnp.float32)
    dw_kernel = scatter_about(key_of[5], (3, 3, EXP), 9 ** -0.5, 2.0, (), jnp.float32)
    w_proj = scatter_about(key_of[6], (EXP, D), EXP ** -0.5, 0.109375)
    w_qkv = scatter_about(key_of[7], (D, 3 * D), D ** -0.5, 0.21875)
    w_out = scatter_about(key_of[8], (D, D), D ** -0.5, 0.21875)
    rel_bias = draw_rel_bias(jax.random.fold_in(key_of[10], 71), 0)
    return {"expanded": expanded, "stream": stream, "land": land, "polar": polar, "land_shift": land_shift, "dw_kernel": dw_kernel, "w_proj": w_proj, "w_qkv": w_qkv, "w_out": w_out, "rel_bias": rel_bias}


eps = 1e-05

def reference(expanded, stream, land, polar, land_shift, dw_kernel, w_proj, w_qkv, w_out, rel_bias):
    rows_all, cols_all, width_exp = expanded.shape
    width = stream.shape[2]
    heads = rel_bias.shape[0]
    head_dim = width // heads
    padded = jnp.pad(expanded, ((1, 1), (0, 0), (0, 0)))
    padded = jnp.concatenate([padded[:, -1:], padded, padded[:, :1]], axis=1)

    def mix_row(index):
        band = lax.dynamic_slice_in_dim(padded, index, 3, 0).astype(jnp.float32)
        land_row = lax.dynamic_index_in_dim(land, index, 0, keepdims=False)
        filtered = land_row[:, None].astype(jnp.float32) * land_shift[None, :]
        for row_tap in range(3):
            for col_tap in range(3):
                filtered = filtered + band[row_tap, col_tap:col_tap + cols_all] * dw_kernel[row_tap, col_tap]
        activated = jax.nn.gelu(filtered).astype(jnp.bfloat16)
        base = lax.dynamic_index_in_dim(stream, index, 0, keepdims=False).astype(jnp.float32)
        return (base + jnp.dot(activated, w_proj, preferred_element_type=jnp.float32)).astype(jnp.bfloat16)
    mixed = lax.map(mix_row, jnp.arange(rows_all, dtype=jnp.int32))
    flat = mixed.reshape(-1, width).astype(jnp.float32)
    centre = lax.optimization_barrier(jnp.mean(flat, axis=1, keepdims=True))
    centred = flat - centre
    spread = lax.optimization_barrier(jnp.mean(centred * centred, axis=1, keepdims=True))
    normed = (centred * lax.rsqrt(spread + eps)).astype(jnp.bfloat16)
    qkv = jnp.dot(normed, w_qkv, preferred_element_type=jnp.float32).astype(jnp.bfloat16)
    strip = rows_all // GRID
    band_cols = cols_all // GRID

    def split(block):
        return block.reshape(GRID, strip, GRID, band_cols, heads, head_dim)
    queries = split(qkv[:, :width])
    keys = split(qkv[:, width:2 * width])
    values = split(qkv[:, 2 * width:])
    lat_query = np.arange(GRID)[:, None, None, None]
    lon_query = np.arange(GRID)[None, :, None, None]
    lat_key = np.arange(GRID)[None, None, :, None]
    lon_key = np.arange(GRID)[None, None, None, :]
    lat_index = lat_key - lat_query + GRID - 1 + 0 * lon_key + 0 * lon_query
    lon_index = (lon_key - lon_query) % GRID + 0 * lat_key + 0 * lat_query
    table = rel_bias[:, lat_index, lon_index]
    cap_rows = polar.reshape(GRID, strip)

    def attend_strip(index):
        query_part = lax.dynamic_index_in_dim(queries, index, 1, keepdims=False).astype(jnp.float32)
        key_part = lax.dynamic_index_in_dim(keys, index, 1, keepdims=False).astype(jnp.float32)
        value_part = lax.dynamic_index_in_dim(values, index, 1, keepdims=False).astype(jnp.float32)
        allowed = lax.dynamic_index_in_dim(cap_rows, index, 1, keepdims=False) == 0
        scores = jnp.einsum('mnchd,kjchd->chmnkj', query_part, key_part) * head_dim ** (-0.5) + table[None]
        scores = jnp.where(allowed[None, None, None, None, :, None], scores, -1e+30)
        shape_full = scores.shape
        scores = scores.reshape(shape_full[:4] + (GRID * GRID,))
        peak = lax.optimization_barrier(jnp.max(scores, axis=-1, keepdims=True))
        weights = jnp.exp(scores - peak)
        probs = (weights / lax.optimization_barrier(jnp.sum(weights, axis=-1, keepdims=True))).astype(jnp.bfloat16)
        probs = probs.reshape(shape_full).astype(jnp.float32)
        attended = jnp.einsum('chmnkj,kjchd->mnchd', probs, value_part)
        return attended.astype(jnp.bfloat16)
    pieces = lax.map(attend_strip, jnp.arange(strip, dtype=jnp.int32))
    attended = jnp.transpose(pieces, (1, 0, 2, 3, 4, 5)).reshape(rows_all * cols_all, width)
    result = flat.astype(jnp.float32) + jnp.dot(attended, w_out, preferred_element_type=jnp.float32)
    return result.astype(jnp.bfloat16).reshape(rows_all, cols_all, width)
```

```python
import functools

import jax
import jax.numpy as jnp
import numpy as np
from jax import lax
from jax.experimental import pallas as pl
from jax.experimental.pallas import tpu as pltpu
from jax.sharding import PartitionSpec as P

GRID = 8
LANES = 128
NEVER = -1e30

eps = 1e-05


def orders(rows, cols, lats):
    halves = GRID // lats
    packs = cols // GRID
    per = halves * packs
    count = rows * cols
    home = np.zeros((2 * count, 2 * count), np.float32)
    away = np.zeros((2 * count, 2 * count), np.float32)
    for lat in range(lats):
        for n in range(GRID):
            for a in range(halves):
                for g in range(packs):
                    for part in range(2):
                        slot = (lat * GRID + n) * 2 * per + part * per + a * packs + g
                        own = (a * lats + lat) * cols + g * GRID + n
                        group = (g * GRID + lat * halves + a) * GRID + n
                        home[slot, part * count + own] = 1
                        away[slot, part * count + group] = 1
    return home, away


def edge_picks(rows, cols):
    picks = np.zeros((6 * 8, rows * cols), np.float32)
    for r in range(rows):
        picks[r, r * cols] = 1
        picks[8 + r, r * cols + cols - 1] = 1
    picks[16, 0] = 1
    picks[24, cols - 1] = 1
    picks[32, (rows - 1) * cols] = 1
    picks[40, rows * cols - 1] = 1
    return picks


def kernel(
    lats,
    lons,
    heads,
    expanded,
    stream,
    w_proj,
    w_qkv,
    w_out,
    polar_in,
    land_in,
    shift_in,
    taps_in,
    table_in,
    picks_in,
    home_in,
    home_t_in,
    away_in,
    away_t_in,
    out,
    ext,
    edges,
    corners,
    side,
    corner_in,
    stream_v,
    wp,
    wq,
    wo,
    partial,
    total,
    lands,
    grid_table,
    mixed,
    turned,
    bias,
    qkv,
    attended,
    sent1,
    came1,
    sent2,
    came2,
    order_v,
    polar,
    land,
    shift,
    taps,
    table,
    picks,
    local_sem,
    halo_send,
    halo_recv,
    send1,
    recv1,
    send2,
    recv2,
    own_sem,
):
    rows, cols, width_exp = expanded.shape
    width = stream.shape[1]
    half = width // 2
    count = rows * cols
    team = lats * GRID
    stride = lons // GRID
    strip = lats
    head_dim = width // heads
    lat = lax.axis_index("lat")
    lon = lax.axis_index("lon")
    member = lon // stride
    spot = lon % stride
    me = lat * GRID + member

    north, south = lax.rem(lat + lats - 1, lats), lax.rem(lat + 1, lats)
    west, east = lax.rem(lon + lons - 1, lons), lax.rem(lon + 1, lons)
    hops = [
        (i, j)
        for j in sorted(range(GRID), key=lambda j: -min(j, GRID - j))
        for i in sorted(range(lats), key=lambda i: -min(i, lats - i))
        if (i, j) != (0, 0)
    ]

    def ahead(at, by, length):
        to = at + by
        return jnp.where(to >= length, to - length, to)

    def reach(i, j):
        return ahead(lat, i, lats), ahead(member, j, GRID)

    barrier = pltpu.get_barrier_semaphore()
    for i, j in hops:
        to_lat, to_member = reach(i, j)
        pl.semaphore_signal(
            barrier, inc=1, device_id={"lat": to_lat, "lon": to_member * stride + spot}
        )
    greeted = team - 1
    if stride > 1:
        for i in (north, lat, south):
            for j in (west, east):
                pl.semaphore_signal(barrier, inc=1, device_id={"lat": i, "lon": j})
        greeted += 6

    loads = [
        pltpu.make_async_copy(expanded, ext.at[pl.ds(1, rows)], local_sem.at[0]),
        pltpu.make_async_copy(stream, stream_v, local_sem.at[1]),
        pltpu.make_async_copy(w_proj, wp, local_sem.at[2]),
        pltpu.make_async_copy(w_qkv, wq, local_sem.at[3]),
        pltpu.make_async_copy(w_out, wo, local_sem.at[4]),
    ]
    for k, order in enumerate((home_in, away_t_in, away_in, home_t_in)):
        loads.append(pltpu.make_async_copy(order, order_v.at[k], local_sem.at[5 + k]))
    small = [
        pltpu.make_async_copy(src, dst, local_sem.at[9 + k])
        for k, (src, dst) in enumerate(
            [
                (picks_in, picks),
                (taps_in, taps),
                (shift_in, shift),
                (land_in, land),
                (table_in, table),
                (polar_in, polar),
            ]
        )
    ]
    for load in [loads[0]] + small + loads[2:3] + loads[1:2] + loads[3:]:
        load.start()

    loads[0].wait()
    for load in small:
        load.wait()
    block = ext[1 : rows + 1].reshape(count, width_exp)
    picked = jnp.dot(picks[...], block, preferred_element_type=jnp.float32)
    edges[0] = picked[0:rows].astype(jnp.bfloat16)
    edges[1] = picked[8 : 8 + rows].astype(jnp.bfloat16)
    for c in range(4):
        corners[c] = picked[16 + 8 * c : 17 + 8 * c]
    pl.semaphore_wait(barrier, greeted)

    def halo(src, dst, k, i, j):
        return pltpu.make_async_remote_copy(
            src_ref=src,
            dst_ref=dst,
            send_sem=halo_send.at[k],
            recv_sem=halo_recv.at[k],
            device_id={"lat": i, "lon": j},
        )

    side_halos = [
        halo(edges.at[1], side.at[0], 2, lat, east),
        halo(edges.at[0], side.at[1], 3, lat, west),
    ]
    south_halos = [
        halo(corners.at[3], corner_in.at[0], 4, south, east),
        halo(corners.at[2], corner_in.at[1], 5, south, west),
        halo(expanded.at[rows - 1], ext.at[0], 0, south, lon),
    ]
    north_halos = [
        halo(corners.at[1], corner_in.at[2], 6, north, east),
        halo(corners.at[0], corner_in.at[3], 7, north, west),
        halo(expanded.at[0], ext.at[rows + 1], 1, north, lon),
    ]
    for copy in side_halos:
        copy.start()

    @pl.when(lat < lats - 1)
    def _():
        for copy in south_halos:
            copy.start()

    @pl.when(lat > 0)
    def _():
        for copy in north_halos:
            copy.start()

    @pl.when(lat == 0)
    def _():
        ext[0] = jnp.zeros_like(ext[0])
        corner_in[0:2] = jnp.zeros_like(corner_in[0:2])

    @pl.when(lat == lats - 1)
    def _():
        ext[rows + 1] = jnp.zeros_like(ext[0])
        corner_in[2:4] = jnp.zeros_like(corner_in[0:2])

    pick = lax.broadcasted_iota(jnp.int32, (cols, cols), 0)
    eye = (pick == lax.broadcasted_iota(jnp.int32, (cols, cols), 1)).astype(jnp.bfloat16)
    land_t = lax.dot_general(
        eye,
        land[...].astype(jnp.float32).astype(jnp.bfloat16),
        (((1,), (1,)), ((), ())),
        preferred_element_type=jnp.float32,
    )
    for r in range(rows):
        lands[r] = jnp.broadcast_to(land_t[:, r : r + 1], (cols, LANES))
    token = lax.broadcasted_iota(jnp.int32, (cols, LANES), 0)

    def beside(x):
        before = jnp.where(token == 0, 0.0, pltpu.roll(x, 1, axis=0))
        after = jnp.where(token == cols - 1, 0.0, pltpu.roll(x, cols - 1, axis=0))
        return before, x, after

    def filter_own(c, _):
        at = pl.ds(pl.multiple_of(c * LANES, LANES), LANES)
        kern = [[taps[a, b : b + 1, at] for b in range(3)] for a in range(3)]
        shift_row = shift[:, at]
        near = {}
        for e in range(1, rows + 2):
            if e <= rows:
                near[e] = beside(ext[e, :, at].astype(jnp.float32))
            r = e - 2
            if r < 0:
                continue
            total_r = lands[r] * shift_row
            for a in range(3):
                if r + a in near:
                    for b in range(3):
                        total_r = total_r + near[r + a][b] * kern[a][b]
            partial[r, :, at] = total_r
        return 0

    lax.fori_loop(0, width_exp // LANES, filter_own, 0)

    for copy in side_halos:
        copy.wait()

    @pl.when(lat < lats - 1)
    def _():
        for copy in south_halos:
            copy.wait_send()
        for copy in north_halos:
            copy.wait_recv()

    @pl.when(lat > 0)
    def _():
        for copy in north_halos:
            copy.wait_send()
        for copy in south_halos:
            copy.wait_recv()

    loads[2].wait()
    step = 2 * LANES
    row_of = lax.broadcasted_iota(jnp.int32, (rows, LANES), 0)

    def column(k, at, kern, b):
        x = side[k, :, at].astype(jnp.float32)
        above = corner_in[k, :, at]
        below = corner_in[2 + k, :, at]
        up = jnp.where(row_of == 0, above, pltpu.roll(x, 1, axis=0))
        down = jnp.where(row_of == rows - 1, below, pltpu.roll(x, rows - 1, axis=0))
        return up * kern[0][b] + x * kern[1][b] + down * kern[2][b]

    def finish_filter(c, _):
        pieces = []
        for block_at in range(2):
            at = pl.ds(pl.multiple_of(c * step + block_at * LANES, LANES), LANES)
            kern = [[taps[a, b : b + 1, at] for b in range(3)] for a in range(3)]
            west_sum = column(0, at, kern, 0)
            east_sum = column(1, at, kern, 2)
            done = []
            for r in range(rows):
                total_r = partial[r, :, at]
                if r == 0 or r == rows - 1:
                    e, a = (0, 0) if r == 0 else (rows + 1, 2)
                    far = beside(ext[e, :, at].astype(jnp.float32))
                    for b in range(3):
                        total_r = total_r + far[b] * kern[a][b]
                total_r = total_r + jnp.where(token == 0, west_sum[r : r + 1], 0.0)
                total_r = total_r + jnp.where(token == cols - 1, east_sum[r : r + 1], 0.0)
                done.append(jax.nn.gelu(total_r).astype(jnp.bfloat16))
            pieces.append(jnp.concatenate(done, axis=0))
        weight = wp[pl.ds(pl.multiple_of(c * step, step), step), :]
        term = jnp.dot(
            jnp.concatenate(pieces, axis=1), weight, preferred_element_type=jnp.float32
        )
        total[...] = total[...] + term
        return 0

    total[...] = jnp.zeros_like(total)
    lax.fori_loop(0, width_exp // step, finish_filter, 0)

    loads[1].wait()
    projected = total[...]
    whole = (stream_v[...].astype(jnp.float32) + projected).astype(jnp.bfloat16)
    whole = whole.astype(jnp.float32)
    mixed[...] = whole
    centred = whole - jnp.mean(whole, axis=1, keepdims=True)
    spread = jnp.mean(centred * centred, axis=1, keepdims=True)
    normed = centred * lax.rsqrt(spread + eps)

    def pack(order, x):
        x = x.astype(jnp.bfloat16)
        stacked = jnp.concatenate([x[:, :half], x[:, half:]], axis=0)
        slabs = jnp.dot(order, stacked, preferred_element_type=jnp.float32)
        return slabs.reshape(team, 2 * count // team, half).astype(jnp.bfloat16)

    def unpack(order_t, slabs):
        flat = slabs.astype(jnp.float32).reshape(2 * count, half).astype(jnp.bfloat16)
        stacked = jnp.dot(order_t, flat, preferred_element_type=jnp.float32)
        return jnp.concatenate([stacked[:count], stacked[count:]], axis=1).astype(jnp.bfloat16)

    def exchange(src, dst, sends, recvs, own_at, meanwhile):
        own = pltpu.make_async_copy(src.at[me], dst.at[me], own_sem.at[own_at])
        own.start()
        for i, j in hops:
            to_lat, to_member = reach(i, j)
            pltpu.make_async_remote_copy(
                src_ref=src.at[to_lat * GRID + to_member],
                dst_ref=dst.at[me],
                send_sem=sends,
                recv_sem=recvs,
                device_id={"lat": to_lat, "lon": to_member * stride + spot},
            ).start()
        if meanwhile is not None:
            meanwhile()
        own.wait()
        others = pl.ds(0, team - 1)
        pltpu.make_async_copy(dst.at[others], dst.at[others], recvs).wait()
        pltpu.make_async_copy(src.at[others], src.at[others], sends).wait()

    def spread_bias():
        lane = lax.broadcasted_iota(jnp.int32, (heads, LANES), 1)
        grid_table[...] = jnp.zeros_like(grid_table)
        grid_table[: table.shape[0], :heads] = table[...]
        flat = grid_table[...].T[:heads]
        for n in range(GRID):
            near = flat if n == 0 else pltpu.roll(flat, n, axis=1)
            far = pltpu.roll(flat, LANES - GRID + n, axis=1)
            turned[:, n, :] = jnp.where((lane & (GRID - 1)) >= n, near, far)
        packs = count // (GRID * GRID)
        lane8 = lax.broadcasted_iota(jnp.int32, (GRID, LANES), 1)
        capped = jnp.zeros((GRID, LANES), jnp.int32)
        for m in range(GRID):
            capped = jnp.where(
                (lane8 & (GRID * GRID - 1)) // GRID == m, polar[m * strip + lat], capped
            )
        open_key = capped == 0

        def fill(h, _):
            own = turned[h]
            for g in range(packs):
                lo, hi = g * GRID * GRID, (g + 1) * GRID * GRID
                allowed = open_key & (lane8 >= lo) & (lane8 < hi)
                for m in range(GRID):
                    by = (lo + LANES - (GRID - 1 - m) * GRID) % LANES
                    moved = own if by == 0 else pltpu.roll(own, by, axis=1)
                    at = (g * GRID + m) * GRID
                    bias[h, at : at + GRID, :] = jnp.where(allowed, moved, NEVER)
            return 0

        lax.fori_loop(0, heads, fill, 0)

    for load in loads[5:]:
        load.wait()
    sent1[...] = pack(order_v[0], normed)
    exchange(sent1, came1, send1, recv1, 0, spread_bias)
    tokens = unpack(order_v[1], came1[...])
    loads[3].wait()
    qkv[...] = jnp.dot(tokens, wq[...], preferred_element_type=jnp.float32).astype(jnp.bfloat16)

    per = LANES // head_dim
    lane_head = lax.broadcasted_iota(jnp.int32, (count, LANES), 1) // head_dim
    scale = head_dim ** (-0.5)
    for p in range(heads // per):
        q = qkv[:, p * LANES : (p + 1) * LANES]
        k = qkv[:, width + p * LANES : width + (p + 1) * LANES]
        v = qkv[:, 2 * width + p * LANES : 2 * width + (p + 1) * LANES]
        zero = jnp.zeros_like(q)
        joined = jnp.zeros((count, LANES), jnp.float32)
        for h in range(per):
            mine = lane_head == h
            scores = lax.dot_general(
                jnp.where(mine, q, zero),
                k,
                (((1,), (1,)), ((), ())),
                preferred_element_type=jnp.float32,
            )
            scores = scores * scale + bias[p * per + h]
            weights = jnp.exp(scores - jnp.max(scores, axis=1, keepdims=True))
            probs = weights / jnp.sum(weights, axis=1, keepdims=True)
            joined = joined + jnp.dot(
                probs.astype(jnp.bfloat16),
                jnp.where(mine, v, zero),
                preferred_element_type=jnp.float32,
            )
        attended[:, p * LANES : (p + 1) * LANES] = joined.astype(jnp.bfloat16)

    sent2[...] = pack(order_v[2], attended[...])
    exchange(sent2, came2, send2, recv2, 1, None)
    back = unpack(order_v[3], came2[...])
    loads[4].wait()
    result = mixed[...] + jnp.dot(back, wo[...], preferred_element_type=jnp.float32)
    out[...] = result.astype(jnp.bfloat16)


def local(lats, lons, expanded, stream, land, polar, land_shift, dw_kernel, w_proj, w_qkv, w_out, rel_bias):
    rows, cols, width_exp = expanded.shape
    width = stream.shape[2]
    heads = rel_bias.shape[0]
    count = rows * cols
    team = lats * GRID
    assert rows * lats == GRID * lats and count == LANES and GRID * (2 * GRID - 1) <= LANES
    table = jnp.transpose(rel_bias, (1, 2, 0)).reshape(-1, heads)
    home, away = orders(rows, cols, lats)
    bf16, f32 = jnp.bfloat16, jnp.float32
    slabs = (team, 2 * count // team, width // 2)
    any_ = pl.BlockSpec(memory_space=pl.ANY)
    vmem = pl.BlockSpec(memory_space=pltpu.VMEM)
    dma = pltpu.SemaphoreType.DMA
    result = pl.pallas_call(
        functools.partial(kernel, lats, lons, heads),
        out_shape=pltpu.VMEM((count, width), bf16),
        in_specs=[any_] * 15,
        out_specs=vmem,
        scratch_shapes=[
            pltpu.VMEM((rows + 2, cols, width_exp), bf16),
            pltpu.VMEM((2, rows, width_exp), bf16),
            pltpu.VMEM((4, 1, width_exp), f32),
            pltpu.VMEM((2, rows, width_exp), bf16),
            pltpu.VMEM((4, 1, width_exp), f32),
            pltpu.VMEM((count, width), bf16),
            pltpu.VMEM(w_proj.shape, bf16),
            pltpu.VMEM(w_qkv.shape, bf16),
            pltpu.VMEM(w_out.shape, bf16),
            pltpu.VMEM((rows, cols, width_exp), f32),
            pltpu.VMEM((count, width), f32),
            pltpu.VMEM((rows, cols, LANES), f32),
            pltpu.VMEM((LANES, LANES), f32),
            pltpu.VMEM((count, width), f32),
            pltpu.VMEM((heads, GRID, LANES), f32),
            pltpu.VMEM((heads, count, LANES), f32),
            pltpu.VMEM((count, 3 * width), bf16),
            pltpu.VMEM((count, width), bf16),
            pltpu.VMEM(slabs, bf16),
            pltpu.VMEM(slabs, bf16),
            pltpu.VMEM(slabs, bf16),
            pltpu.VMEM(slabs, bf16),
            pltpu.VMEM((4,) + home.shape, bf16),
            pltpu.SMEM(polar.shape, jnp.int32),
            pltpu.VMEM(land.shape, jnp.int32),
            pltpu.VMEM((1, width_exp), f32),
            pltpu.VMEM(dw_kernel.shape, f32),
            pltpu.VMEM(table.shape, f32),
            pltpu.VMEM((6 * 8, count), bf16),
            dma((15,)),
            dma((8,)),
            dma((8,)),
            dma,
            dma,
            dma,
            dma,
            dma((2,)),
        ],
        compiler_params=pltpu.CompilerParams(collective_id=0, has_side_effects=True),
        name="section",
    )(
        expanded,
        stream.reshape(count, width),
        w_proj,
        w_qkv,
        w_out,
        polar,
        land,
        land_shift[None],
        dw_kernel,
        table,
        jnp.asarray(edge_picks(rows, cols), bf16),
        jnp.asarray(home, bf16),
        jnp.asarray(home.T, bf16),
        jnp.asarray(away, bf16),
        jnp.asarray(away.T, bf16),
    )
    return result.reshape(rows, cols, width)


def solution(mesh):
    in_specs = (P("lat", "lon", None),) * 2 + (P("lat", "lon"),) + (P(),) * 7
    out_specs = P("lat", "lon", None)
    body = functools.partial(local, mesh.shape["lat"], mesh.shape["lon"])
    return jax.shard_map(body, mesh=mesh, in_specs=in_specs, out_specs=out_specs, check_vma=False)
```

```python
import functools

import jax
import jax.numpy as jnp
import numpy as np
from jax import lax
from jax.experimental import pallas as pl
from jax.experimental.pallas import tpu as pltpu
from jax.sharding import PartitionSpec as P

GRID = 8
LANES = 128
NEVER = -1e30

eps = 1e-05


def orders(rows, cols, lats):
    halves = GRID // lats
    packs = cols // GRID
    per = halves * packs
    count = rows * cols
    home = np.zeros((2 * count, 2 * count), np.float32)
    away = np.zeros((2 * count, 2 * count), np.float32)
    for lat in range(lats):
        for n in range(GRID):
            for a in range(halves):
                for g in range(packs):
                    for part in range(2):
                        slot = (lat * GRID + n) * 2 * per + part * per + a * packs + g
                        own = (a * lats + lat) * cols + g * GRID + n
                        group = (g * GRID + lat * halves + a) * GRID + n
                        home[slot, part * count + own] = 1
                        away[slot, part * count + group] = 1
    return home, away


def edge_picks(rows, cols):
    picks = np.zeros((6 * 8, rows * cols), np.float32)
    for r in range(rows):
        picks[r, r * cols] = 1
        picks[8 + r, r * cols + cols - 1] = 1
    picks[16, 0] = 1
    picks[24, cols - 1] = 1
    picks[32, (rows - 1) * cols] = 1
    picks[40, rows * cols - 1] = 1
    return picks


def kernel(
    lats,
    lons,
    heads,
    expanded,
    stream,
    w_proj,
    w_qkv,
    w_out,
    polar_in,
    land_in,
    shift_in,
    taps_in,
    table_in,
    picks_in,
    home_in,
    home_t_in,
    away_in,
    away_t_in,
    out,
    ext,
    edges,
    corners,
    side,
    corner_in,
    stream_v,
    wp,
    wq,
    wo,
    partial,
    total,
    lands,
    grid_table,
    mixed,
    turned,
    bias,
    qkv,
    sent1,
    came1,
    sent2,
    came2,
    order_v,
    polar,
    land,
    shift,
    taps,
    table,
    picks,
    local_sem,
    halo_send,
    halo_recv,
    send1,
    recv1,
    send2,
    recv2,
    own_sem,
):
    rows, cols, width_exp = expanded.shape
    width = stream.shape[1]
    half = width // 2
    count = rows * cols
    team = lats * GRID
    stride = lons // GRID
    strip = lats
    members = GRID * GRID
    packs = count // members
    head_dim = width // heads
    lat = lax.axis_index("lat")
    lon = lax.axis_index("lon")
    member = lon // stride
    spot = lon % stride
    me = lat * GRID + member

    north, south = lax.rem(lat + lats - 1, lats), lax.rem(lat + 1, lats)
    west, east = lax.rem(lon + lons - 1, lons), lax.rem(lon + 1, lons)
    hops = [
        (i, j)
        for j in sorted(range(GRID), key=lambda j: -min(j, GRID - j))
        for i in sorted(range(lats), key=lambda i: -min(i, lats - i))
        if (i, j) != (0, 0)
    ]

    def ahead(at, by, length):
        to = at + by
        return jnp.where(to >= length, to - length, to)

    def reach(i, j):
        return ahead(lat, i, lats), ahead(member, j, GRID)

    barrier = pltpu.get_barrier_semaphore()
    for i, j in hops:
        to_lat, to_member = reach(i, j)
        pl.semaphore_signal(
            barrier, inc=1, device_id={"lat": to_lat, "lon": to_member * stride + spot}
        )
    greeted = team - 1
    if stride > 1:
        for i in (north, lat, south):
            for j in (west, east):
                pl.semaphore_signal(barrier, inc=1, device_id={"lat": i, "lon": j})
        greeted += 6

    loads = [
        pltpu.make_async_copy(expanded, ext.at[pl.ds(1, rows)], local_sem.at[0]),
        pltpu.make_async_copy(stream, stream_v, local_sem.at[1]),
        pltpu.make_async_copy(w_proj, wp, local_sem.at[2]),
        pltpu.make_async_copy(w_qkv, wq, local_sem.at[3]),
        pltpu.make_async_copy(w_out, wo, local_sem.at[4]),
    ]
    for k, order in enumerate((home_in, away_t_in, away_in, home_t_in)):
        loads.append(pltpu.make_async_copy(order, order_v.at[k], local_sem.at[5 + k]))
    small = [
        pltpu.make_async_copy(src, dst, local_sem.at[9 + k])
        for k, (src, dst) in enumerate(
            [
                (picks_in, picks),
                (taps_in, taps),
                (shift_in, shift),
                (land_in, land),
                (table_in, table),
                (polar_in, polar),
            ]
        )
    ]
    for load in [loads[0]] + small + loads[2:3] + loads[1:2] + loads[3:]:
        load.start()

    loads[0].wait()
    for load in small:
        load.wait()
    block = ext[1 : rows + 1].reshape(count, width_exp)
    picked = jnp.dot(picks[...], block, preferred_element_type=jnp.float32)
    edges[0] = picked[0:rows].astype(jnp.bfloat16)
    edges[1] = picked[8 : 8 + rows].astype(jnp.bfloat16)
    for c in range(4):
        corners[c] = picked[16 + 8 * c : 17 + 8 * c]
    pl.semaphore_wait(barrier, greeted)

    def halo(src, dst, k, i, j):
        return pltpu.make_async_remote_copy(
            src_ref=src,
            dst_ref=dst,
            send_sem=halo_send.at[k],
            recv_sem=halo_recv.at[k],
            device_id={"lat": i, "lon": j},
        )

    side_halos = [
        halo(edges.at[1], side.at[0], 2, lat, east),
        halo(edges.at[0], side.at[1], 3, lat, west),
    ]
    south_halos = [
        halo(corners.at[3], corner_in.at[0], 4, south, east),
        halo(corners.at[2], corner_in.at[1], 5, south, west),
        halo(expanded.at[rows - 1], ext.at[0], 0, south, lon),
    ]
    north_halos = [
        halo(corners.at[1], corner_in.at[2], 6, north, east),
        halo(corners.at[0], corner_in.at[3], 7, north, west),
        halo(expanded.at[0], ext.at[rows + 1], 1, north, lon),
    ]
    for copy in side_halos:
        copy.start()

    @pl.when(lat < lats - 1)
    def _():
        for copy in south_halos:
            copy.start()

    @pl.when(lat > 0)
    def _():
        for copy in north_halos:
            copy.start()

    @pl.when(lat == 0)
    def _():
        ext[0] = jnp.zeros_like(ext[0])
        corner_in[0:2] = jnp.zeros_like(corner_in[0:2])

    @pl.when(lat == lats - 1)
    def _():
        ext[rows + 1] = jnp.zeros_like(ext[0])
        corner_in[2:4] = jnp.zeros_like(corner_in[0:2])

    pick = lax.broadcasted_iota(jnp.int32, (cols, cols), 0)
    eye = (pick == lax.broadcasted_iota(jnp.int32, (cols, cols), 1)).astype(jnp.bfloat16)
    land_t = lax.dot_general(
        eye,
        land[...].astype(jnp.float32).astype(jnp.bfloat16),
        (((1,), (1,)), ((), ())),
        preferred_element_type=jnp.float32,
    )
    for r in range(rows):
        lands[r] = jnp.broadcast_to(land_t[:, r : r + 1], (cols, LANES))
    token = lax.broadcasted_iota(jnp.int32, (cols, LANES), 0)

    def beside(x):
        before = jnp.where(token == 0, 0.0, pltpu.roll(x, 1, axis=0))
        after = jnp.where(token == cols - 1, 0.0, pltpu.roll(x, cols - 1, axis=0))
        return before, x, after

    def filter_own(c, _):
        at = pl.ds(pl.multiple_of(c * LANES, LANES), LANES)
        kern = [[taps[a, b : b + 1, at] for b in range(3)] for a in range(3)]
        shift_row = shift[:, at]
        near = {}
        for e in range(1, rows + 2):
            if e <= rows:
                near[e] = beside(ext[e, :, at].astype(jnp.float32))
            r = e - 2
            if r < 0:
                continue
            total_r = lands[r] * shift_row
            for a in range(3):
                if r + a in near:
                    for b in range(3):
                        total_r = total_r + near[r + a][b] * kern[a][b]
            partial[r, :, at] = total_r
        return 0

    lax.fori_loop(0, width_exp // LANES, filter_own, 0)

    for copy in side_halos:
        copy.wait()

    @pl.when(lat < lats - 1)
    def _():
        for copy in south_halos:
            copy.wait_send()
        for copy in north_halos:
            copy.wait_recv()

    @pl.when(lat > 0)
    def _():
        for copy in north_halos:
            copy.wait_send()
        for copy in south_halos:
            copy.wait_recv()

    loads[2].wait()
    step = 2 * LANES
    row_of = lax.broadcasted_iota(jnp.int32, (rows, LANES), 0)

    def column(k, at, kern, b):
        x = side[k, :, at].astype(jnp.float32)
        above = corner_in[k, :, at]
        below = corner_in[2 + k, :, at]
        up = jnp.where(row_of == 0, above, pltpu.roll(x, 1, axis=0))
        down = jnp.where(row_of == rows - 1, below, pltpu.roll(x, rows - 1, axis=0))
        return up * kern[0][b] + x * kern[1][b] + down * kern[2][b]

    def finish_filter(c, _):
        pieces = []
        for block_at in range(2):
            at = pl.ds(pl.multiple_of(c * step + block_at * LANES, LANES), LANES)
            kern = [[taps[a, b : b + 1, at] for b in range(3)] for a in range(3)]
            west_sum = column(0, at, kern, 0)
            east_sum = column(1, at, kern, 2)
            done = []
            for r in range(rows):
                total_r = partial[r, :, at]
                if r == 0 or r == rows - 1:
                    e, a = (0, 0) if r == 0 else (rows + 1, 2)
                    far = beside(ext[e, :, at].astype(jnp.float32))
                    for b in range(3):
                        total_r = total_r + far[b] * kern[a][b]
                total_r = total_r + jnp.where(token == 0, west_sum[r : r + 1], 0.0)
                total_r = total_r + jnp.where(token == cols - 1, east_sum[r : r + 1], 0.0)
                done.append(jax.nn.gelu(total_r).astype(jnp.bfloat16))
            pieces.append(jnp.concatenate(done, axis=0))
        weight = wp[pl.ds(pl.multiple_of(c * step, step), step), :]
        term = jnp.dot(
            jnp.concatenate(pieces, axis=1), weight, preferred_element_type=jnp.float32
        )
        total[...] = total[...] + term
        return 0

    total[...] = jnp.zeros_like(total)
    lax.fori_loop(0, width_exp // step, finish_filter, 0)

    loads[1].wait()
    projected = total[...]
    whole = (stream_v[...].astype(jnp.float32) + projected).astype(jnp.bfloat16)
    whole = whole.astype(jnp.float32)
    mixed[...] = whole
    centred = whole - jnp.mean(whole, axis=1, keepdims=True)
    spread = jnp.mean(centred * centred, axis=1, keepdims=True)
    normed = centred * lax.rsqrt(spread + eps)

    def as_slabs(slabs):
        return slabs.reshape(team, 2 * count // team, slabs.shape[1]).astype(jnp.bfloat16)

    def unpack(order_t, slabs):
        flat = slabs.astype(jnp.float32).reshape(2 * count, slabs.shape[2]).astype(jnp.bfloat16)
        stacked = jnp.dot(order_t, flat, preferred_element_type=jnp.float32)
        return jnp.concatenate([stacked[:count], stacked[count:]], axis=1).astype(jnp.bfloat16)

    def send(src, dst, sends, recvs, own):
        pltpu.make_async_copy(src.at[me], dst.at[me], own).start()
        for i, j in hops:
            to_lat, to_member = reach(i, j)
            pltpu.make_async_remote_copy(
                src_ref=src.at[to_lat * GRID + to_member],
                dst_ref=dst.at[me],
                send_sem=sends,
                recv_sem=recvs,
                device_id={"lat": to_lat, "lon": to_member * stride + spot},
            ).start()

    def arrive(src, dst, sends, recvs, own):
        pltpu.make_async_copy(src.at[me], dst.at[me], own).wait()
        others = pl.ds(0, team - 1)
        pltpu.make_async_copy(dst.at[others], dst.at[others], recvs).wait()
        pltpu.make_async_copy(src.at[others], src.at[others], sends).wait()

    def spread_bias():
        lane = lax.broadcasted_iota(jnp.int32, (heads, LANES), 1)
        grid_table[...] = jnp.zeros_like(grid_table)
        for a in range(2 * GRID - 1):
            for b in range(GRID):
                to = (2 * GRID - 2 - a) * GRID + (GRID - b) % GRID
                grid_table[to : to + 1, :heads] = table[a * GRID + b : a * GRID + b + 1]
        flat = grid_table[...].T[:heads]
        for n in range(GRID):
            near = flat if n == 0 else pltpu.roll(flat, n, axis=1)
            far = pltpu.roll(flat, LANES - GRID + n, axis=1)
            turned[:, n, :] = jnp.where((lane & (GRID - 1)) >= n, near, far)
        lane8 = lax.broadcasted_iota(jnp.int32, (GRID, LANES), 1)
        open_key = [
            jnp.full((GRID, LANES), polar[m * strip + lat], jnp.int32) == 0 for m in range(GRID)
        ]

        def fill(h, _):
            own = turned[h]
            for m in range(GRID):
                moved = None
                for g in range(packs):
                    by = (g * members + LANES - (GRID - 1 - m) * GRID) % LANES
                    here = own if by == 0 else pltpu.roll(own, by, axis=1)
                    moved = here if g == 0 else jnp.where(lane8 >= g * members, here, moved)
                bias[h, m * GRID : (m + 1) * GRID, :] = jnp.where(open_key[m], moved, NEVER)
            return 0

        lax.fori_loop(0, heads, fill, 0)

    for load in loads[5:]:
        load.wait()
    normed = normed.astype(jnp.bfloat16)
    stacked = jnp.concatenate([normed[:, :half], normed[:, half:]], axis=0)
    sent1[...] = as_slabs(jnp.dot(order_v[0], stacked, preferred_element_type=jnp.float32))
    first = (sent1, came1, send1, recv1, own_sem.at[0])
    send(*first)
    spread_bias()
    loads[3].wait()
    arrive(*first)
    tokens = unpack(order_v[1], came1[...])
    qkv[...] = jnp.dot(tokens, wq[...], preferred_element_type=jnp.float32).astype(jnp.bfloat16)

    per = LANES // head_dim
    lane_head = lax.broadcasted_iota(jnp.int32, (count, LANES), 1) // head_dim
    query_lane = lax.broadcasted_iota(jnp.int32, (members, LANES), 1) // members
    ones = jnp.ones((16, LANES), jnp.bfloat16)
    scale = head_dim ** (-0.5)

    def attend(p):
        q = qkv[:, p * LANES : (p + 1) * LANES]
        k = qkv[:, width + p * LANES : width + (p + 1) * LANES]
        v = qkv[:, 2 * width + p * LANES : 2 * width + (p + 1) * LANES]
        v_t = v.T
        keys = jnp.concatenate([k[g * members : (g + 1) * members] for g in range(packs)], axis=1)
        zero = jnp.zeros_like(q)
        none = jnp.zeros((members, LANES), jnp.bfloat16)
        queries = []
        for h in range(per):
            own = jnp.where(lane_head == h, q, zero)
            for g in range(packs):
                part = own[g * members : (g + 1) * members]
                queries.append(
                    jnp.concatenate([part if f == g else none for f in range(packs)], axis=1)
                )
        scores_all = lax.dot_general(
            keys,
            jnp.concatenate(queries, axis=0),
            (((1,), (1,)), ((), ())),
            preferred_element_type=jnp.float32,
        )
        done = []
        for h in range(0, per, 2):
            spread = []
            for e in (h, h + 1):
                scores = scores_all[:, e * count : (e + 1) * count] * scale + bias[p * per + e]
                weights = jnp.exp(scores - jnp.max(scores, axis=0, keepdims=True))
                weights = weights.astype(jnp.bfloat16)
                spread.append(
                    jnp.concatenate(
                        [jnp.where(query_lane == g, weights, none) for g in range(packs)], axis=0
                    )
                )
            summed = jnp.dot(
                jnp.concatenate([v_t[h * head_dim : (h + 2) * head_dim], ones], axis=0),
                jnp.concatenate(spread, axis=1),
                preferred_element_type=jnp.float32,
            )
            for e in range(2):
                mine = summed[:, e * count : (e + 1) * count]
                total_e = mine[2 * head_dim : 2 * head_dim + 1]
                done.append(mine[e * head_dim : (e + 1) * head_dim] * (1.0 / total_e))
        return jnp.concatenate(done, axis=0).astype(jnp.bfloat16)

    chunks = width // (2 * LANES)
    backs = [
        (sent2.at[c], came2.at[c], send2.at[c], recv2.at[c], own_sem.at[1 + c])
        for c in range(chunks)
    ]
    for c in range(chunks):
        pair = jnp.concatenate([attend(2 * c), attend(2 * c + 1)], axis=1)
        sent2[c] = as_slabs(
            lax.dot_general(
                order_v[2], pair, (((1,), (1,)), ((), ())), preferred_element_type=jnp.float32
            )
        )
        send(*backs[c])

    loads[4].wait()
    result = mixed[...]
    for c in range(chunks):
        arrive(*backs[c])
        back = unpack(order_v[3], came2[c])
        result = result + jnp.dot(
            back, wo[2 * c * LANES : 2 * (c + 1) * LANES, :], preferred_element_type=jnp.float32
        )
    out[...] = result.astype(jnp.bfloat16)


def local(lats, lons, expanded, stream, land, polar, land_shift, dw_kernel, w_proj, w_qkv, w_out, rel_bias):
    rows, cols, width_exp = expanded.shape
    width = stream.shape[2]
    heads = rel_bias.shape[0]
    count = rows * cols
    team = lats * GRID
    assert rows * lats == GRID * lats and count == LANES and GRID * (2 * GRID - 1) <= LANES
    table = jnp.transpose(rel_bias, (1, 2, 0)).reshape(-1, heads)
    home, away = orders(rows, cols, lats)
    bf16, f32 = jnp.bfloat16, jnp.float32
    slabs = (team, 2 * count // team, width // 2)
    chunks = width // (2 * LANES)
    pieces = (chunks, team, 2 * count // team, LANES)
    any_ = pl.BlockSpec(memory_space=pl.ANY)
    vmem = pl.BlockSpec(memory_space=pltpu.VMEM)
    dma = pltpu.SemaphoreType.DMA
    result = pl.pallas_call(
        functools.partial(kernel, lats, lons, heads),
        out_shape=pltpu.VMEM((count, width), bf16),
        in_specs=[any_] * 15,
        out_specs=vmem,
        scratch_shapes=[
            pltpu.VMEM((rows + 2, cols, width_exp), bf16),
            pltpu.VMEM((2, rows, width_exp), bf16),
            pltpu.VMEM((4, 1, width_exp), f32),
            pltpu.VMEM((2, rows, width_exp), bf16),
            pltpu.VMEM((4, 1, width_exp), f32),
            pltpu.VMEM((count, width), bf16),
            pltpu.VMEM(w_proj.shape, bf16),
            pltpu.VMEM(w_qkv.shape, bf16),
            pltpu.VMEM(w_out.shape, bf16),
            pltpu.VMEM((rows, cols, width_exp), f32),
            pltpu.VMEM((count, width), f32),
            pltpu.VMEM((rows, cols, LANES), f32),
            pltpu.VMEM((LANES, LANES), f32),
            pltpu.VMEM((count, width), f32),
            pltpu.VMEM((heads, GRID, LANES), f32),
            pltpu.VMEM((heads, GRID * GRID, LANES), f32),
            pltpu.VMEM((count, 3 * width), bf16),
            pltpu.VMEM(slabs, bf16),
            pltpu.VMEM(slabs, bf16),
            pltpu.VMEM(pieces, bf16),
            pltpu.VMEM(pieces, bf16),
            pltpu.VMEM((4,) + home.shape, bf16),
            pltpu.SMEM(polar.shape, jnp.int32),
            pltpu.VMEM(land.shape, jnp.int32),
            pltpu.VMEM((1, width_exp), f32),
            pltpu.VMEM(dw_kernel.shape, f32),
            pltpu.VMEM(table.shape, f32),
            pltpu.VMEM((6 * 8, count), bf16),
            dma((15,)),
            dma((8,)),
            dma((8,)),
            dma,
            dma,
            dma((chunks,)),
            dma((chunks,)),
            dma((1 + chunks,)),
        ],
        compiler_params=pltpu.CompilerParams(collective_id=0, has_side_effects=True),
        name="section",
    )(
        expanded,
        stream.reshape(count, width),
        w_proj,
        w_qkv,
        w_out,
        polar,
        land,
        land_shift[None],
        dw_kernel,
        table,
        jnp.asarray(edge_picks(rows, cols), bf16),
        jnp.asarray(home, bf16),
        jnp.asarray(home.T, bf16),
        jnp.asarray(away, bf16),
        jnp.asarray(away.T, bf16),
    )
    return result.reshape(rows, cols, width)


def solution(mesh):
    in_specs = (P("lat", "lon", None),) * 2 + (P("lat", "lon"),) + (P(),) * 7
    out_specs = P("lat", "lon", None)
    body = functools.partial(local, mesh.shape["lat"], mesh.shape["lon"])
    return jax.shard_map(body, mesh=mesh, in_specs=in_specs, out_specs=out_specs, check_vma=False)
```

```python
import functools

import jax
import jax.numpy as jnp
import numpy as np
from jax import lax
from jax.experimental import pallas as pl
from jax.experimental.pallas import tpu as pltpu
from jax.sharding import PartitionSpec as P

GRID = 8
LANES = 128
NEVER = -1e30

eps = 1e-05


def orders(rows, cols, lats):
    halves = GRID // lats
    packs = cols // GRID
    per = halves * packs
    count = rows * cols
    home = np.zeros((2 * count, 2 * count), np.float32)
    away = np.zeros((2 * count, 2 * count), np.float32)
    for lat in range(lats):
        for n in range(GRID):
            for a in range(halves):
                for g in range(packs):
                    for part in range(2):
                        slot = (lat * GRID + n) * 2 * per + part * per + a * packs + g
                        own = (a * lats + lat) * cols + g * GRID + n
                        group = (g * GRID + lat * halves + a) * GRID + n
                        home[slot, part * count + own] = 1
                        away[slot, part * count + group] = 1
    return home, away


def rim(rows, cols):
    west = [r * cols for r in range(rows)]
    east = [r * cols + cols - 1 for r in range(rows)]
    first = list(range(cols))
    last = list(range((rows - 1) * cols, rows * cols))
    return west + east + first + last


def rim_tables(rows, cols, home):
    count = rows * cols
    tokens = rim(rows, cols)
    picks = np.zeros((len(tokens), count), np.float32)
    spread = np.zeros((count, len(tokens)), np.float32)
    rim_home = np.zeros((2 * count, 2 * len(tokens)), np.float32)
    inner_home = home.copy()
    for at, token in enumerate(tokens):
        picks[at, token] = 1
        if tokens.index(token) == at:
            spread[token, at] = 1
            for part in range(2):
                rim_home[:, part * len(tokens) + at] = home[:, part * count + token]
                inner_home[:, part * count + token] = 0
    keep = [part * count + t for part in range(2) for t in range(cols, count - cols)]
    return picks, spread, rim_home, inner_home[:, keep]


def edge_picks(rows, cols):
    picks = np.zeros((8 * 8, rows * cols), np.float32)
    for r in range(rows):
        for at, c in enumerate((0, 1, cols - 2, cols - 1)):
            picks[8 * at + r, r * cols + c] = 1
    picks[32, 0] = 1
    picks[40, cols - 1] = 1
    picks[48, (rows - 1) * cols] = 1
    picks[56, rows * cols - 1] = 1
    return picks


def kernel(
    lats,
    lons,
    heads,
    expanded,
    stream,
    w_proj,
    w_qkv,
    w_out,
    polar_in,
    land_in,
    shift_in,
    taps_in,
    table_in,
    picks_in,
    inner_home_in,
    rim_home_in,
    home_t_in,
    away_in,
    away_t_in,
    rim_picks_in,
    spread_in,
    out,
    ext,
    edges,
    corners,
    side,
    corner_in,
    stream_v,
    wp,
    wq,
    wo,
    own_cols,
    partial,
    column_partial,
    active,
    rim_active,
    slabs,
    early,
    lands,
    grid_table,
    mixed,
    turned,
    bias,
    qkv,
    sent1,
    came1,
    sent2,
    came2,
    order_v,
    inner_home,
    rim_home,
    rim_picks,
    spread,
    polar,
    land,
    shift,
    taps,
    table,
    picks,
    local_sem,
    halo_send,
    halo_recv,
    send1,
    recv1,
    send2,
    recv2,
    own_sem,
):
    rows, cols, width_exp = expanded.shape
    width = stream.shape[1]
    half = width // 2
    count = rows * cols
    team = lats * GRID
    stride = lons // GRID
    strip = lats
    members = GRID * GRID
    packs = count // members
    head_dim = width // heads
    lat = lax.axis_index("lat")
    lon = lax.axis_index("lon")
    member = lon // stride
    spot = lon % stride
    me = lat * GRID + member

    north, south = lax.rem(lat + lats - 1, lats), lax.rem(lat + 1, lats)
    west, east = lax.rem(lon + lons - 1, lons), lax.rem(lon + 1, lons)
    hops = [
        (i, j)
        for j in sorted(range(GRID), key=lambda j: -min(j, GRID - j))
        for i in sorted(range(lats), key=lambda i: -min(i, lats - i))
        if (i, j) != (0, 0)
    ]

    def ahead(at, by, length):
        to = at + by
        return jnp.where(to >= length, to - length, to)

    def reach(i, j):
        return ahead(lat, i, lats), ahead(member, j, GRID)

    barrier = pltpu.get_barrier_semaphore()
    for i, j in hops:
        to_lat, to_member = reach(i, j)
        pl.semaphore_signal(
            barrier, inc=1, device_id={"lat": to_lat, "lon": to_member * stride + spot}
        )
    greeted = team - 1
    if stride > 1:
        for i in (north, lat, south):
            for j in (west, east):
                pl.semaphore_signal(barrier, inc=1, device_id={"lat": i, "lon": j})
        greeted += 6

    loads = [
        pltpu.make_async_copy(expanded, ext.at[pl.ds(1, rows)], local_sem.at[0]),
        pltpu.make_async_copy(stream, stream_v, local_sem.at[1]),
        pltpu.make_async_copy(w_proj, wp, local_sem.at[2]),
        pltpu.make_async_copy(w_qkv, wq, local_sem.at[3]),
        pltpu.make_async_copy(w_out, wo, local_sem.at[4]),
    ]
    for k, order in enumerate((away_t_in, away_in, home_t_in)):
        loads.append(pltpu.make_async_copy(order, order_v.at[k], local_sem.at[5 + k]))
    small = [
        pltpu.make_async_copy(src, dst, local_sem.at[8 + k])
        for k, (src, dst) in enumerate(
            [
                (picks_in, picks),
                (taps_in, taps),
                (shift_in, shift),
                (land_in, land),
                (table_in, table),
                (polar_in, polar),
                (inner_home_in, inner_home),
                (rim_home_in, rim_home),
                (rim_picks_in, rim_picks),
                (spread_in, spread),
            ]
        )
    ]
    for load in [loads[0]] + small[:4]:
        load.start()

    loads[0].wait()
    small[0].wait()
    for load in loads[2:3] + loads[1:2] + small[4:] + loads[3:]:
        load.start()
    block = ext[1 : rows + 1].reshape(count, width_exp)
    picked = jnp.dot(picks[...], block, preferred_element_type=jnp.float32)
    edges[0] = picked[0:rows].astype(jnp.bfloat16)
    edges[1] = picked[24 : 24 + rows].astype(jnp.bfloat16)
    for c in range(4):
        corners[c] = picked[32 + 8 * c : 33 + 8 * c]
        own_cols[c] = picked[8 * c : 8 * c + rows]
    pl.semaphore_wait(barrier, greeted)

    def halo(src, dst, k, i, j):
        return pltpu.make_async_remote_copy(
            src_ref=src,
            dst_ref=dst,
            send_sem=halo_send.at[k],
            recv_sem=halo_recv.at[k],
            device_id={"lat": i, "lon": j},
        )

    side_halos = [
        halo(edges.at[1], side.at[0], 2, lat, east),
        halo(edges.at[0], side.at[1], 3, lat, west),
    ]
    south_halos = [
        halo(corners.at[3], corner_in.at[0], 4, south, east),
        halo(corners.at[2], corner_in.at[1], 5, south, west),
        halo(expanded.at[rows - 1], ext.at[0], 0, south, lon),
    ]
    north_halos = [
        halo(corners.at[1], corner_in.at[2], 6, north, east),
        halo(corners.at[0], corner_in.at[3], 7, north, west),
        halo(expanded.at[0], ext.at[rows + 1], 1, north, lon),
    ]
    for copy in side_halos:
        copy.start()

    @pl.when(lat < lats - 1)
    def _():
        for copy in south_halos:
            copy.start()

    @pl.when(lat > 0)
    def _():
        for copy in north_halos:
            copy.start()

    @pl.when(lat == 0)
    def _():
        ext[0] = jnp.zeros_like(ext[0])
        corner_in[0:2] = jnp.zeros_like(corner_in[0:2])

    @pl.when(lat == lats - 1)
    def _():
        ext[rows + 1] = jnp.zeros_like(ext[0])
        corner_in[2:4] = jnp.zeros_like(corner_in[0:2])

    for load in small[1:4]:
        load.wait()
    pick = lax.broadcasted_iota(jnp.int32, (cols, cols), 0)
    eye = (pick == lax.broadcasted_iota(jnp.int32, (cols, cols), 1)).astype(jnp.bfloat16)
    land_t = lax.dot_general(
        eye,
        land[...].astype(jnp.float32).astype(jnp.bfloat16),
        (((1,), (1,)), ((), ())),
        preferred_element_type=jnp.float32,
    )
    for r in range(rows):
        lands[r] = jnp.broadcast_to(land_t[:, r : r + 1], (cols, LANES))
    token = lax.broadcasted_iota(jnp.int32, (cols, LANES), 0)
    row_of = lax.broadcasted_iota(jnp.int32, (rows, LANES), 0)
    land_f = land[...].astype(jnp.float32)
    land_sides = [
        jnp.broadcast_to(land_f[:, c : c + 1], (rows, LANES)) for c in (0, cols - 1)
    ]

    def beside(x):
        before = jnp.where(token == 0, 0.0, pltpu.roll(x, 1, axis=0))
        after = jnp.where(token == cols - 1, 0.0, pltpu.roll(x, cols - 1, axis=0))
        return before, x, after

    def filter_own(c, _):
        at = pl.ds(pl.multiple_of(c * LANES, LANES), LANES)
        kern = [[taps[a, b : b + 1, at] for b in range(3)] for a in range(3)]
        shift_row = shift[:, at]
        near = {}
        for e in range(1, rows + 2):
            if e <= rows:
                near[e] = beside(ext[e, :, at].astype(jnp.float32))
            r = e - 2
            if r < 0:
                continue
            total_r = lands[r] * shift_row
            for a in range(3):
                if r + a in near:
                    for b in range(3):
                        total_r = total_r + near[r + a][b] * kern[a][b]
            if r == 0 or r == rows - 1:
                partial[0 if r == 0 else 1, :, at] = total_r
            else:
                active[(r - 1) * cols : r * cols, at] = jax.nn.gelu(total_r).astype(jnp.bfloat16)
        for k, (mid, other, b) in enumerate(((0, 1, 2), (3, 2, 0))):
            total_k = land_sides[k] * shift_row
            for at_col, tap in ((mid, 1), (other, b)):
                x = own_cols[at_col, :, at]
                up = jnp.where(row_of == 0, 0.0, pltpu.roll(x, 1, axis=0))
                down = jnp.where(row_of == rows - 1, 0.0, pltpu.roll(x, rows - 1, axis=0))
                total_k = total_k + up * kern[0][tap] + x * kern[1][tap] + down * kern[2][tap]
            column_partial[k, :, at] = total_k
        return 0

    lax.fori_loop(0, width_exp // LANES, filter_own, 0)

    def as_slabs(x):
        return x.reshape(team, 2 * count // team, x.shape[1]).astype(jnp.bfloat16)

    def unpack(order_t, slabs):
        flat = slabs.astype(jnp.float32).reshape(2 * count, slabs.shape[2]).astype(jnp.bfloat16)
        stacked = jnp.dot(order_t, flat, preferred_element_type=jnp.float32)
        return jnp.concatenate([stacked[:count], stacked[count:]], axis=1).astype(jnp.bfloat16)

    def send(src, dst, sends, recvs, inner=None):
        for i, j in hops:
            to_lat, to_member = reach(i, j)
            copy = pltpu.make_async_remote_copy(
                src_ref=src.at[to_lat * GRID + to_member],
                dst_ref=dst.at[me],
                send_sem=sends,
                recv_sem=recvs,
                device_id={"lat": to_lat, "lon": to_member * stride + spot},
            )
            if inner is None:
                copy.start()
            else:
                amid = (
                    (to_lat > 0)
                    & (to_lat < lats - 1)
                    & (to_member > 0)
                    & (to_member < GRID - 1)
                )

                @pl.when(amid if inner else jnp.logical_not(amid))
                def _():
                    copy.start()

    def arrive(src, dst, sends, recvs, own):
        pltpu.make_async_copy(src.at[me], dst.at[me], own).wait()
        others = pl.ds(0, team - 1)
        pltpu.make_async_copy(dst.at[others], dst.at[others], recvs).wait()
        pltpu.make_async_copy(src.at[others], src.at[others], sends).wait()

    loads[2].wait()
    loads[1].wait()
    for load in small[4:]:
        load.wait()

    def mix(base, acts):
        projected = jnp.dot(acts, wp[...], preferred_element_type=jnp.float32)
        whole = (base + projected).astype(jnp.bfloat16)
        wide = whole.astype(jnp.float32)
        centred = wide - jnp.mean(wide, axis=1, keepdims=True)
        var = jnp.mean(centred * centred, axis=1, keepdims=True)
        normed = (centred * lax.rsqrt(var + eps)).astype(jnp.bfloat16)
        return whole, jnp.concatenate([normed[:, :half], normed[:, half:]], axis=0)

    inner_base = stream_v[cols : count - cols].astype(jnp.float32)
    inner_mixed, inner_stacked = mix(inner_base, active[...])
    mixed[cols : count - cols] = inner_mixed.astype(jnp.float32)
    slabs[...] = jnp.dot(inner_home[...], inner_stacked, preferred_element_type=jnp.float32)
    early[...] = as_slabs(slabs[...])
    send(early, came1, send1, recv1, True)
    rim_base = jnp.dot(rim_picks[...], stream_v[...], preferred_element_type=jnp.float32)

    for copy in side_halos:
        copy.wait()

    @pl.when(lat < lats - 1)
    def _():
        for copy in south_halos:
            copy.wait_send()
        for copy in north_halos:
            copy.wait_recv()

    @pl.when(lat > 0)
    def _():
        for copy in north_halos:
            copy.wait_send()
        for copy in south_halos:
            copy.wait_recv()

    def column(k, at, kern, b):
        x = side[k, :, at].astype(jnp.float32)
        above = corner_in[k, :, at]
        below = corner_in[2 + k, :, at]
        up = jnp.where(row_of == 0, above, pltpu.roll(x, 1, axis=0))
        down = jnp.where(row_of == rows - 1, below, pltpu.roll(x, rows - 1, axis=0))
        return up * kern[0][b] + x * kern[1][b] + down * kern[2][b]

    def filter_rim(c, _):
        at = pl.ds(pl.multiple_of(c * LANES, LANES), LANES)
        kern = [[taps[a, b : b + 1, at] for b in range(3)] for a in range(3)]
        sums = [column_partial[k, :, at] + column(k, at, kern, 2 * k) for k in range(2)]
        for k, (e, a, row) in enumerate(((0, 0, 0), (rows + 1, 2, rows - 1))):
            x = ext[e, :, at].astype(jnp.float32)
            far = beside(x)
            total_r = partial[k, :, at]
            for b in range(3):
                total_r = total_r + far[b] * kern[a][b]
            sums.append(total_r)
            west_far = x[0:1] * kern[a][1] + x[1:2] * kern[a][2]
            east_far = x[cols - 2 : cols - 1] * kern[a][0] + x[cols - 1 : cols] * kern[a][1]
            sums[0] = sums[0] + jnp.where(row_of == row, west_far, 0.0)
            sums[1] = sums[1] + jnp.where(row_of == row, east_far, 0.0)
        rim_active[:, at] = jax.nn.gelu(jnp.concatenate(sums, axis=0)).astype(jnp.bfloat16)
        return 0

    lax.fori_loop(0, width_exp // LANES, filter_rim, 0)
    rim_mixed, rim_stacked = mix(rim_base, rim_active[...])

    def spread_bias():
        lane = lax.broadcasted_iota(jnp.int32, (heads, LANES), 1)
        grid_table[...] = jnp.zeros_like(grid_table)
        for a in range(2 * GRID - 1):
            for b in range(GRID):
                to = (2 * GRID - 2 - a) * GRID + (GRID - b) % GRID
                grid_table[to : to + 1, :heads] = table[a * GRID + b : a * GRID + b + 1]
        flat = grid_table[...].T[:heads]
        for n in range(GRID):
            near = flat if n == 0 else pltpu.roll(flat, n, axis=1)
            far = pltpu.roll(flat, LANES - GRID + n, axis=1)
            turned[:, n, :] = jnp.where((lane & (GRID - 1)) >= n, near, far)
        lane8 = lax.broadcasted_iota(jnp.int32, (GRID, LANES), 1)
        open_key = [
            jnp.full((GRID, LANES), polar[m * strip + lat], jnp.int32) == 0 for m in range(GRID)
        ]

        def fill(h, _):
            own = turned[h]
            for m in range(GRID):
                moved = None
                for g in range(packs):
                    by = (g * members + LANES - (GRID - 1 - m) * GRID) % LANES
                    here = own if by == 0 else pltpu.roll(own, by, axis=1)
                    moved = here if g == 0 else jnp.where(lane8 >= g * members, here, moved)
                bias[h, m * GRID : (m + 1) * GRID, :] = jnp.where(open_key[m], moved, NEVER)
            return 0

        lax.fori_loop(0, heads, fill, 0)

    for load in loads[5:]:
        load.wait()
    sent1[...] = as_slabs(
        slabs[...] + jnp.dot(rim_home[...], rim_stacked, preferred_element_type=jnp.float32)
    )
    first = (sent1, came1, send1, recv1, own_sem.at[0])
    pltpu.make_async_copy(sent1.at[me], came1.at[me], own_sem.at[0]).start()
    send(sent1, came1, send1, recv1, False)
    spread_bias()
    fixed = jnp.dot(spread[...], rim_mixed, preferred_element_type=jnp.float32)
    mixed[0:cols] = fixed[0:cols]
    mixed[count - cols : count] = fixed[count - cols : count]
    column_of = lax.broadcasted_iota(jnp.int32, (count - 2 * cols, width), 0) & (cols - 1)
    mixed[cols : count - cols] = jnp.where(
        (column_of == 0) | (column_of == cols - 1),
        fixed[cols : count - cols],
        mixed[cols : count - cols],
    )
    loads[3].wait()
    arrive(*first)
    tokens = unpack(order_v[0], came1[...])

    per = LANES // head_dim
    lane_head = lax.broadcasted_iota(jnp.int32, (count, LANES), 1) // head_dim
    query_lane = lax.broadcasted_iota(jnp.int32, (members, LANES), 1) // members
    ones = jnp.ones((16, LANES), jnp.bfloat16)
    scale = head_dim ** (-0.5)

    def attend(p):
        q, k, v = (
            qkv[:, part * width + p * LANES : part * width + (p + 1) * LANES] for part in range(3)
        )
        v_t = v.T
        keys = jnp.concatenate([k[g * members : (g + 1) * members] for g in range(packs)], axis=1)
        zero = jnp.zeros_like(q)
        none = jnp.zeros((members, LANES), jnp.bfloat16)
        queries = []
        for h in range(per):
            own = jnp.where(lane_head == h, q, zero)
            for g in range(packs):
                part = own[g * members : (g + 1) * members]
                queries.append(
                    jnp.concatenate([part if f == g else none for f in range(packs)], axis=1)
                )
        scores_all = lax.dot_general(
            keys,
            jnp.concatenate(queries, axis=0),
            (((1,), (1,)), ((), ())),
            preferred_element_type=jnp.float32,
        )
        done = []
        for h in range(0, per, 2):
            spread = []
            for e in (h, h + 1):
                scores = scores_all[:, e * count : (e + 1) * count] * scale + bias[p * per + e]
                weights = jnp.exp(scores - jnp.max(scores, axis=0, keepdims=True))
                weights = weights.astype(jnp.bfloat16)
                spread.append(
                    jnp.concatenate(
                        [jnp.where(query_lane == g, weights, none) for g in range(packs)], axis=0
                    )
                )
            summed = jnp.dot(
                jnp.concatenate([v_t[h * head_dim : (h + 2) * head_dim], ones], axis=0),
                jnp.concatenate(spread, axis=1),
                preferred_element_type=jnp.float32,
            )
            for e in range(2):
                mine = summed[:, e * count : (e + 1) * count]
                total_e = mine[2 * head_dim : 2 * head_dim + 1]
                done.append(mine[e * head_dim : (e + 1) * head_dim] * (1.0 / total_e))
        return jnp.concatenate(done, axis=0).astype(jnp.bfloat16)

    chunks = width // (2 * LANES)
    backs = [
        (sent2.at[c], came2.at[c], send2.at[c], recv2.at[c], own_sem.at[1 + c])
        for c in range(chunks)
    ]
    for c in range(chunks):
        for part in range(3):
            at = part * width + 2 * c * LANES
            qkv[:, at : at + 2 * LANES] = jnp.dot(
                tokens, wq[:, at : at + 2 * LANES], preferred_element_type=jnp.float32
            ).astype(jnp.bfloat16)
        pair = jnp.concatenate([attend(2 * c), attend(2 * c + 1)], axis=1)
        sent2[c] = as_slabs(
            lax.dot_general(
                order_v[1], pair, (((1,), (1,)), ((), ())), preferred_element_type=jnp.float32
            )
        )
        pltpu.make_async_copy(sent2.at[c, me], came2.at[c, me], own_sem.at[1 + c]).start()
        send(*backs[c][:4])

    loads[4].wait()
    result = mixed[...]
    for c in range(chunks):
        arrive(*backs[c])
        back = unpack(order_v[2], came2[c])
        result = result + jnp.dot(
            back, wo[2 * c * LANES : 2 * (c + 1) * LANES, :], preferred_element_type=jnp.float32
        )
    out[...] = result.astype(jnp.bfloat16)


def local(lats, lons, expanded, stream, land, polar, land_shift, dw_kernel, w_proj, w_qkv, w_out, rel_bias):
    rows, cols, width_exp = expanded.shape
    width = stream.shape[2]
    heads = rel_bias.shape[0]
    count = rows * cols
    team = lats * GRID
    assert rows * lats == GRID * lats and count == LANES and GRID * (2 * GRID - 1) <= LANES
    table = jnp.transpose(rel_bias, (1, 2, 0)).reshape(-1, heads)
    home, away = orders(rows, cols, lats)
    rim_picks, spread, rim_home, inner_home = rim_tables(rows, cols, home)
    rim_count = len(rim_picks)
    assert cols & (cols - 1) == 0
    bf16, f32 = jnp.bfloat16, jnp.float32
    slabs = (team, 2 * count // team, width // 2)
    chunks = width // (2 * LANES)
    pieces = (chunks, team, 2 * count // team, LANES)
    any_ = pl.BlockSpec(memory_space=pl.ANY)
    vmem = pl.BlockSpec(memory_space=pltpu.VMEM)
    dma = pltpu.SemaphoreType.DMA
    result = pl.pallas_call(
        functools.partial(kernel, lats, lons, heads),
        out_shape=pltpu.VMEM((count, width), bf16),
        in_specs=[any_] * 18,
        out_specs=vmem,
        scratch_shapes=[
            pltpu.VMEM((rows + 2, cols, width_exp), bf16),
            pltpu.VMEM((2, rows, width_exp), bf16),
            pltpu.VMEM((4, 1, width_exp), f32),
            pltpu.VMEM((2, rows, width_exp), bf16),
            pltpu.VMEM((4, 1, width_exp), f32),
            pltpu.VMEM((count, width), bf16),
            pltpu.VMEM(w_proj.shape, bf16),
            pltpu.VMEM(w_qkv.shape, bf16),
            pltpu.VMEM(w_out.shape, bf16),
            pltpu.VMEM((4, rows, width_exp), f32),
            pltpu.VMEM((2, cols, width_exp), f32),
            pltpu.VMEM((2, rows, width_exp), f32),
            pltpu.VMEM((count - 2 * cols, width_exp), bf16),
            pltpu.VMEM((rim_count, width_exp), bf16),
            pltpu.VMEM((2 * count, width // 2), f32),
            pltpu.VMEM(slabs, bf16),
            pltpu.VMEM((rows, cols, LANES), f32),
            pltpu.VMEM((LANES, LANES), f32),
            pltpu.VMEM((count, width), f32),
            pltpu.VMEM((heads, GRID, LANES), f32),
            pltpu.VMEM((heads, GRID * GRID, LANES), f32),
            pltpu.VMEM((count, 3 * width), bf16),
            pltpu.VMEM(slabs, bf16),
            pltpu.VMEM(slabs, bf16),
            pltpu.VMEM(pieces, bf16),
            pltpu.VMEM(pieces, bf16),
            pltpu.VMEM((3,) + home.shape, bf16),
            pltpu.VMEM(inner_home.shape, bf16),
            pltpu.VMEM(rim_home.shape, bf16),
            pltpu.VMEM(rim_picks.shape, bf16),
            pltpu.VMEM(spread.shape, bf16),
            pltpu.SMEM(polar.shape, jnp.int32),
            pltpu.VMEM(land.shape, jnp.int32),
            pltpu.VMEM((1, width_exp), f32),
            pltpu.VMEM(dw_kernel.shape, f32),
            pltpu.VMEM(table.shape, f32),
            pltpu.VMEM((8 * 8, count), bf16),
            dma((18,)),
            dma((8,)),
            dma((8,)),
            dma,
            dma,
            dma((chunks,)),
            dma((chunks,)),
            dma((1 + chunks,)),
        ],
        compiler_params=pltpu.CompilerParams(collective_id=0, has_side_effects=True),
        name="section",
    )(
        expanded,
        stream.reshape(count, width),
        w_proj,
        w_qkv,
        w_out,
        polar,
        land,
        land_shift[None],
        dw_kernel,
        table,
        jnp.asarray(edge_picks(rows, cols), bf16),
        jnp.asarray(inner_home, bf16),
        jnp.asarray(rim_home, bf16),
        jnp.asarray(home.T, bf16),
        jnp.asarray(away, bf16),
        jnp.asarray(away.T, bf16),
        jnp.asarray(rim_picks, bf16),
        jnp.asarray(spread, bf16),
    )
    return result.reshape(rows, cols, width)


def solution(mesh):
    in_specs = (P("lat", "lon", None),) * 2 + (P("lat", "lon"),) + (P(),) * 7
    out_specs = P("lat", "lon", None)
    body = functools.partial(local, mesh.shape["lat"], mesh.shape["lon"])
    return jax.shard_map(body, mesh=mesh, in_specs=in_specs, out_specs=out_specs, check_vma=False)
```

```python
import functools

import jax
import jax.numpy as jnp
import numpy as np
from jax import lax
from jax.experimental import pallas as pl
from jax.experimental.pallas import tpu as pltpu
from jax.sharding import PartitionSpec as P

GRID = 8
LANES = 128
NEVER = -1e30

eps = 1e-05


def orders(rows, cols, lats):
    halves = GRID // lats
    packs = cols // GRID
    per = halves * packs
    count = rows * cols
    home = np.zeros((2 * count, 2 * count), np.float32)
    away = np.zeros((2 * count, 2 * count), np.float32)
    for lat in range(lats):
        for n in range(GRID):
            for a in range(halves):
                for g in range(packs):
                    for part in range(2):
                        slot = (lat * GRID + n) * 2 * per + part * per + a * packs + g
                        own = (a * lats + lat) * cols + g * GRID + n
                        group = (g * GRID + lat * halves + a) * GRID + n
                        home[slot, part * count + own] = 1
                        away[slot, part * count + group] = 1
    return home, away


def rim(rows, cols):
    west = [r * cols for r in range(rows)]
    east = [r * cols + cols - 1 for r in range(rows)]
    first = list(range(cols))
    last = list(range((rows - 1) * cols, rows * cols))
    return west + east + first + last


def rim_tables(rows, cols, home):
    count = rows * cols
    tokens = rim(rows, cols)
    picks = np.zeros((len(tokens), count), np.float32)
    spread = np.zeros((count, len(tokens)), np.float32)
    rim_home = np.zeros((2 * count, 2 * len(tokens)), np.float32)
    inner_home = home.copy()
    for at, token in enumerate(tokens):
        picks[at, token] = 1
        if tokens.index(token) == at:
            spread[token, at] = 1
            for part in range(2):
                rim_home[:, part * len(tokens) + at] = home[:, part * count + token]
                inner_home[:, part * count + token] = 0
    keep = [part * count + t for part in range(2) for t in range(cols, count - cols)]
    return picks, spread, rim_home, inner_home[:, keep]


def edge_picks(rows, cols):
    picks = np.zeros((10 * 8, rows * cols), np.float32)
    for r in range(rows):
        for at, c in ((0, 0), (1, cols - 1), (6, 0), (7, 1), (8, cols - 2), (9, cols - 1)):
            picks[8 * at + r, r * cols + c] = 1
    picks[16, 0] = 1
    picks[24, cols - 1] = 1
    picks[32, (rows - 1) * cols] = 1
    picks[40, rows * cols - 1] = 1
    return picks


def kernel(
    lats,
    lons,
    heads,
    expanded,
    stream,
    w_proj,
    w_qkv,
    w_out,
    polar_in,
    land_in,
    shift_in,
    taps_in,
    table_in,
    picks_in,
    inner_home_in,
    rim_home_in,
    home_t_in,
    away_in,
    away_t_in,
    rim_picks_in,
    spread_in,
    out,
    ext,
    edges,
    corners,
    side,
    corner_in,
    stream_v,
    wp,
    wq,
    wo,
    own_cols,
    partial,
    column_partial,
    active,
    rim_active,
    rim_total,
    slabs,
    early,
    lands,
    grid_table,
    mixed,
    turned,
    bias,
    qkv,
    sent1,
    came1,
    sent2,
    came2,
    order_v,
    inner_home,
    rim_home,
    rim_picks,
    spread,
    polar,
    land,
    shift,
    taps,
    table,
    picks,
    local_sem,
    halo_send,
    halo_recv,
    send1,
    recv1,
    send2,
    recv2,
    own_sem,
):
    rows, cols, width_exp = expanded.shape
    width = stream.shape[1]
    half = width // 2
    count = rows * cols
    team = lats * GRID
    stride = lons // GRID
    strip = lats
    members = GRID * GRID
    packs = count // members
    head_dim = width // heads
    lat = lax.axis_index("lat")
    lon = lax.axis_index("lon")
    member = lon // stride
    spot = lon % stride
    me = lat * GRID + member

    north, south = lax.rem(lat + lats - 1, lats), lax.rem(lat + 1, lats)
    west, east = lax.rem(lon + lons - 1, lons), lax.rem(lon + 1, lons)
    hops = [
        (i, j)
        for j in sorted(range(GRID), key=lambda j: -min(j, GRID - j))
        for i in sorted(range(lats), key=lambda i: -min(i, lats - i))
        if (i, j) != (0, 0)
    ]

    def ahead(at, by, length):
        to = at + by
        return jnp.where(to >= length, to - length, to)

    def reach(i, j):
        return ahead(lat, i, lats), ahead(member, j, GRID)

    loads = [
        pltpu.make_async_copy(expanded, ext.at[pl.ds(1, rows)], local_sem.at[0]),
        pltpu.make_async_copy(stream, stream_v, local_sem.at[1]),
        pltpu.make_async_copy(w_proj, wp, local_sem.at[2]),
        pltpu.make_async_copy(w_qkv, wq, local_sem.at[3]),
        pltpu.make_async_copy(w_out, wo, local_sem.at[4]),
    ]
    for k, order in enumerate((away_t_in, away_in, home_t_in)):
        loads.append(pltpu.make_async_copy(order, order_v.at[k], local_sem.at[5 + k]))
    small = [
        pltpu.make_async_copy(src, dst, local_sem.at[8 + k])
        for k, (src, dst) in enumerate(
            [
                (picks_in, picks),
                (taps_in, taps),
                (shift_in, shift),
                (land_in, land),
                (table_in, table),
                (polar_in, polar),
                (inner_home_in, inner_home),
                (rim_home_in, rim_home),
                (rim_picks_in, rim_picks),
                (spread_in, spread),
            ]
        )
    ]
    for load in [loads[0]] + small[:4]:
        load.start()

    barrier = pltpu.get_barrier_semaphore()
    for i, j in hops:
        to_lat, to_member = reach(i, j)
        pl.semaphore_signal(
            barrier, inc=1, device_id={"lat": to_lat, "lon": to_member * stride + spot}
        )
    greeted = team - 1
    if stride > 1:
        for i in (north, lat, south):
            for j in (west, east):
                pl.semaphore_signal(barrier, inc=1, device_id={"lat": i, "lon": j})
        greeted += 6


    loads[0].wait()
    small[0].wait()
    for load in loads[2:3] + loads[1:2] + small[4:] + loads[3:]:
        load.start()
    block = ext[1 : rows + 1].reshape(count, width_exp)
    picked = jnp.dot(picks[0:48], block, preferred_element_type=jnp.float32)
    edges[0] = picked[0:rows].astype(jnp.bfloat16)
    edges[1] = picked[8 : 8 + rows].astype(jnp.bfloat16)
    for c in range(4):
        corners[c] = picked[16 + 8 * c : 17 + 8 * c]
    pl.semaphore_wait(barrier, greeted)

    def halo(src, dst, k, i, j):
        return pltpu.make_async_remote_copy(
            src_ref=src,
            dst_ref=dst,
            send_sem=halo_send.at[k],
            recv_sem=halo_recv.at[k],
            device_id={"lat": i, "lon": j},
        )

    side_halos = [
        halo(edges.at[1], side.at[0], 2, lat, east),
        halo(edges.at[0], side.at[1], 3, lat, west),
    ]
    south_halos = [
        halo(corners.at[3], corner_in.at[0], 4, south, east),
        halo(corners.at[2], corner_in.at[1], 5, south, west),
        halo(expanded.at[rows - 1], ext.at[0], 0, south, lon),
    ]
    north_halos = [
        halo(corners.at[1], corner_in.at[2], 6, north, east),
        halo(corners.at[0], corner_in.at[3], 7, north, west),
        halo(expanded.at[0], ext.at[rows + 1], 1, north, lon),
    ]
    for copy in side_halos:
        copy.start()

    @pl.when(lat < lats - 1)
    def _():
        for copy in south_halos:
            copy.start()

    @pl.when(lat > 0)
    def _():
        for copy in north_halos:
            copy.start()

    @pl.when(lat == 0)
    def _():
        ext[0] = jnp.zeros_like(ext[0])
        corner_in[0:2] = jnp.zeros_like(corner_in[0:2])

    @pl.when(lat == lats - 1)
    def _():
        ext[rows + 1] = jnp.zeros_like(ext[0])
        corner_in[2:4] = jnp.zeros_like(corner_in[0:2])

    picked = jnp.dot(picks[48:80], block, preferred_element_type=jnp.float32)
    for c in range(4):
        own_cols[c] = picked[8 * c : 8 * c + rows]
    for load in small[1:4]:
        load.wait()
    pick = lax.broadcasted_iota(jnp.int32, (cols, cols), 0)
    eye = (pick == lax.broadcasted_iota(jnp.int32, (cols, cols), 1)).astype(jnp.bfloat16)
    land_t = lax.dot_general(
        eye,
        land[...].astype(jnp.float32).astype(jnp.bfloat16),
        (((1,), (1,)), ((), ())),
        preferred_element_type=jnp.float32,
    )
    for r in range(rows):
        lands[r] = jnp.broadcast_to(land_t[:, r : r + 1], (cols, LANES))
    token = lax.broadcasted_iota(jnp.int32, (cols, LANES), 0)
    row_of = lax.broadcasted_iota(jnp.int32, (rows, LANES), 0)
    land_f = land[...].astype(jnp.float32)
    land_sides = [
        jnp.broadcast_to(land_f[:, c : c + 1], (rows, LANES)) for c in (0, cols - 1)
    ]

    def beside(x):
        before = jnp.where(token == 0, 0.0, pltpu.roll(x, 1, axis=0))
        after = jnp.where(token == cols - 1, 0.0, pltpu.roll(x, cols - 1, axis=0))
        return before, x, after

    def filter_own(c, _):
        at = pl.ds(pl.multiple_of(c * LANES, LANES), LANES)
        kern = [[taps[a, b : b + 1, at] for b in range(3)] for a in range(3)]
        shift_row = shift[:, at]
        near = {}
        for e in range(1, rows + 2):
            if e <= rows:
                near[e] = beside(ext[e, :, at].astype(jnp.float32))
            r = e - 2
            if r < 0:
                continue
            total_r = lands[r] * shift_row
            for a in range(3):
                if r + a in near:
                    for b in range(3):
                        total_r = total_r + near[r + a][b] * kern[a][b]
            if r == 0 or r == rows - 1:
                partial[0 if r == 0 else 1, :, at] = total_r
            else:
                active[(r - 1) * cols : r * cols, at] = jax.nn.gelu(total_r).astype(jnp.bfloat16)
        for k, (mid, other, b) in enumerate(((0, 1, 2), (3, 2, 0))):
            total_k = land_sides[k] * shift_row
            for at_col, tap in ((mid, 1), (other, b)):
                x = own_cols[at_col, :, at]
                up = jnp.where(row_of == 0, 0.0, pltpu.roll(x, 1, axis=0))
                down = jnp.where(row_of == rows - 1, 0.0, pltpu.roll(x, rows - 1, axis=0))
                total_k = total_k + up * kern[0][tap] + x * kern[1][tap] + down * kern[2][tap]
            column_partial[k, :, at] = total_k
        return 0

    lax.fori_loop(0, width_exp // LANES, filter_own, 0)

    def as_slabs(x):
        return x.reshape(team, 2 * count // team, x.shape[1]).astype(jnp.bfloat16)

    def unpack(order_t, slabs):
        flat = slabs.astype(jnp.float32).reshape(2 * count, slabs.shape[2]).astype(jnp.bfloat16)
        stacked = jnp.dot(order_t, flat, preferred_element_type=jnp.float32)
        return jnp.concatenate([stacked[:count], stacked[count:]], axis=1).astype(jnp.bfloat16)

    def send(src, dst, sends, recvs, inner=None):
        for i, j in hops:
            to_lat, to_member = reach(i, j)
            copy = pltpu.make_async_remote_copy(
                src_ref=src.at[to_lat * GRID + to_member],
                dst_ref=dst.at[me],
                send_sem=sends,
                recv_sem=recvs,
                device_id={"lat": to_lat, "lon": to_member * stride + spot},
            )
            if inner is None:
                copy.start()
            else:
                amid = (
                    (to_lat > 0)
                    & (to_lat < lats - 1)
                    & (to_member > 0)
                    & (to_member < GRID - 1)
                )

                @pl.when(amid if inner else jnp.logical_not(amid))
                def _():
                    copy.start()

    def arrive(src, dst, sends, recvs, own):
        pltpu.make_async_copy(src.at[me], dst.at[me], own).wait()
        others = pl.ds(0, team - 1)
        pltpu.make_async_copy(dst.at[others], dst.at[others], recvs).wait()
        pltpu.make_async_copy(src.at[others], src.at[others], sends).wait()

    loads[2].wait()
    loads[1].wait()
    for load in small[4:]:
        load.wait()

    def mix(base, projected):
        whole = (base + projected).astype(jnp.bfloat16)
        wide = whole.astype(jnp.float32)
        centred = wide - jnp.mean(wide, axis=1, keepdims=True)
        var = jnp.mean(centred * centred, axis=1, keepdims=True)
        normed = (centred * lax.rsqrt(var + eps)).astype(jnp.bfloat16)
        return whole, jnp.concatenate([normed[:, :half], normed[:, half:]], axis=0)

    inner_base = stream_v[cols : count - cols].astype(jnp.float32)
    inner_mixed, inner_stacked = mix(
        inner_base, jnp.dot(active[...], wp[...], preferred_element_type=jnp.float32)
    )
    mixed[cols : count - cols] = inner_mixed.astype(jnp.float32)
    slabs[...] = jnp.dot(inner_home[...], inner_stacked, preferred_element_type=jnp.float32)
    early[...] = as_slabs(slabs[...])
    send(early, came1, send1, recv1, True)
    rim_base = jnp.dot(rim_picks[...], stream_v[...], preferred_element_type=jnp.float32)

    for copy in side_halos:
        copy.wait()

    @pl.when(lat < lats - 1)
    def _():
        for copy in south_halos:
            copy.wait_send()
        for copy in north_halos:
            copy.wait_recv()

    @pl.when(lat > 0)
    def _():
        for copy in north_halos:
            copy.wait_send()
        for copy in south_halos:
            copy.wait_recv()

    def column(k, at, kern, b):
        x = side[k, :, at].astype(jnp.float32)
        above = corner_in[k, :, at]
        below = corner_in[2 + k, :, at]
        up = jnp.where(row_of == 0, above, pltpu.roll(x, 1, axis=0))
        down = jnp.where(row_of == rows - 1, below, pltpu.roll(x, rows - 1, axis=0))
        return up * kern[0][b] + x * kern[1][b] + down * kern[2][b]

    def filter_rim(start):
        at = pl.ds(pl.multiple_of(start, LANES), LANES)
        kern = [[taps[a, b : b + 1, at] for b in range(3)] for a in range(3)]
        sums = [column_partial[k, :, at] + column(k, at, kern, 2 * k) for k in range(2)]
        for k, (e, a, row) in enumerate(((0, 0, 0), (rows + 1, 2, rows - 1))):
            x = ext[e, :, at].astype(jnp.float32)
            far = beside(x)
            total_r = partial[k, :, at]
            for b in range(3):
                total_r = total_r + far[b] * kern[a][b]
            sums.append(total_r)
            west_far = x[0:1] * kern[a][1] + x[1:2] * kern[a][2]
            east_far = x[cols - 2 : cols - 1] * kern[a][0] + x[cols - 1 : cols] * kern[a][1]
            sums[0] = sums[0] + jnp.where(row_of == row, west_far, 0.0)
            sums[1] = sums[1] + jnp.where(row_of == row, east_far, 0.0)
        rim_active[:, at] = jax.nn.gelu(jnp.concatenate(sums, axis=0)).astype(jnp.bfloat16)

    steps = 6
    span = width_exp // steps

    def rim_term(c):
        at = pl.ds(pl.multiple_of(c * span, span), span)
        return jnp.dot(rim_active[:, at], wp[at, :], preferred_element_type=jnp.float32)

    def filter_span(c):
        for k in range(span // LANES):
            filter_rim(c * span + k * LANES)

    filter_span(0)
    rim_total[...] = jnp.zeros_like(rim_total)

    def rim_step(c, _):
        rim_total[...] = rim_total[...] + rim_term(c)
        filter_span(c + 1)
        return 0

    lax.fori_loop(0, steps - 1, rim_step, 0)
    rim_mixed, rim_stacked = mix(rim_base, rim_total[...] + rim_term(steps - 1))

    def spread_bias():
        lane = lax.broadcasted_iota(jnp.int32, (heads, LANES), 1)
        grid_table[...] = jnp.zeros_like(grid_table)
        for a in range(2 * GRID - 1):
            for b in range(GRID):
                to = (2 * GRID - 2 - a) * GRID + (GRID - b) % GRID
                grid_table[to : to + 1, :heads] = table[a * GRID + b : a * GRID + b + 1]
        flat = grid_table[...].T[:heads]
        for n in range(GRID):
            near = flat if n == 0 else pltpu.roll(flat, n, axis=1)
            far = pltpu.roll(flat, LANES - GRID + n, axis=1)
            turned[:, n, :] = jnp.where((lane & (GRID - 1)) >= n, near, far)
        lane8 = lax.broadcasted_iota(jnp.int32, (GRID, LANES), 1)
        open_key = [
            jnp.full((GRID, LANES), polar[m * strip + lat], jnp.int32) == 0 for m in range(GRID)
        ]

        def fill(h, _):
            own = turned[h]
            for m in range(GRID):
                moved = None
                for g in range(packs):
                    by = (g * members + LANES - (GRID - 1 - m) * GRID) % LANES
                    here = own if by == 0 else pltpu.roll(own, by, axis=1)
                    moved = here if g == 0 else jnp.where(lane8 >= g * members, here, moved)
                bias[h, m * GRID : (m + 1) * GRID, :] = jnp.where(open_key[m], moved, NEVER)
            return 0

        lax.fori_loop(0, heads, fill, 0)

    for load in loads[5:]:
        load.wait()
    sent1[...] = as_slabs(
        slabs[...] + jnp.dot(rim_home[...], rim_stacked, preferred_element_type=jnp.float32)
    )
    first = (sent1, came1, send1, recv1, own_sem.at[0])
    pltpu.make_async_copy(sent1.at[me], came1.at[me], own_sem.at[0]).start()
    send(sent1, came1, send1, recv1, False)
    spread_bias()
    fixed = jnp.dot(spread[...], rim_mixed, preferred_element_type=jnp.float32)
    mixed[0:cols] = fixed[0:cols]
    mixed[count - cols : count] = fixed[count - cols : count]
    column_of = lax.broadcasted_iota(jnp.int32, (count - 2 * cols, width), 0) & (cols - 1)
    mixed[cols : count - cols] = jnp.where(
        (column_of == 0) | (column_of == cols - 1),
        fixed[cols : count - cols],
        mixed[cols : count - cols],
    )
    loads[3].wait()
    arrive(*first)
    tokens = unpack(order_v[0], came1[...])

    per = LANES // head_dim
    lane_head = lax.broadcasted_iota(jnp.int32, (count, LANES), 1) // head_dim
    query_lane = lax.broadcasted_iota(jnp.int32, (members, LANES), 1) // members
    ones = jnp.ones((16, LANES), jnp.bfloat16)
    scale = head_dim ** (-0.5)

    none = jnp.zeros((members, LANES), jnp.bfloat16)

    def score(p):
        q, k = (
            qkv[:, part * width + p * LANES : part * width + (p + 1) * LANES] for part in range(2)
        )
        keys = jnp.concatenate([k[g * members : (g + 1) * members] for g in range(packs)], axis=1)
        zero = jnp.zeros_like(q)
        queries = []
        for h in range(per):
            own = jnp.where(lane_head == h, q, zero)
            for g in range(packs):
                part = own[g * members : (g + 1) * members]
                queries.append(
                    jnp.concatenate([part if f == g else none for f in range(packs)], axis=1)
                )
        return lax.dot_general(
            keys,
            jnp.concatenate(queries, axis=0),
            (((1,), (1,)), ((), ())),
            preferred_element_type=jnp.float32,
        )

    def soften(p, scores_all):
        spread_all = []
        for h in range(per):
            scores = scores_all[:, h * count : (h + 1) * count] * scale + bias[p * per + h]
            weights = jnp.exp(scores - jnp.max(scores, axis=0, keepdims=True))
            weights = weights.astype(jnp.bfloat16)
            spread_all.append(
                jnp.concatenate(
                    [jnp.where(query_lane == g, weights, none) for g in range(packs)], axis=0
                )
            )
        return spread_all

    def gather(p, spread_all):
        v_t = qkv[:, 2 * width + p * LANES : 2 * width + (p + 1) * LANES].T
        summed = [
            jnp.dot(
                jnp.concatenate([v_t[h * head_dim : (h + 2) * head_dim], ones], axis=0),
                jnp.concatenate(spread_all[h : h + 2], axis=1),
                preferred_element_type=jnp.float32,
            )
            for h in range(0, per, 2)
        ]
        done = []
        for h in range(per):
            e = h % 2
            mine = summed[h // 2][:, e * count : (e + 1) * count]
            total_h = mine[2 * head_dim : 2 * head_dim + 1]
            done.append(mine[e * head_dim : (e + 1) * head_dim] * (1.0 / total_h))
        return jnp.concatenate(done, axis=0).astype(jnp.bfloat16)

    def attend_pair(c):
        pair = (2 * c, 2 * c + 1)
        scored = [score(p) for p in pair]
        softened = [soften(p, x) for p, x in zip(pair, scored)]
        return [gather(p, x) for p, x in zip(pair, softened)]

    chunks = width // (2 * LANES)
    backs = [
        (sent2.at[c], came2.at[c], send2.at[c], recv2.at[c], own_sem.at[1 + c])
        for c in range(chunks)
    ]
    for c in range(chunks):
        for part in range(3):
            at = part * width + 2 * c * LANES
            qkv[:, at : at + 2 * LANES] = jnp.dot(
                tokens, wq[:, at : at + 2 * LANES], preferred_element_type=jnp.float32
            ).astype(jnp.bfloat16)
        pair = jnp.concatenate(attend_pair(c), axis=1)
        sent2[c] = as_slabs(
            lax.dot_general(
                order_v[1], pair, (((1,), (1,)), ((), ())), preferred_element_type=jnp.float32
            )
        )
        pltpu.make_async_copy(sent2.at[c, me], came2.at[c, me], own_sem.at[1 + c]).start()
        send(*backs[c][:4])

    loads[4].wait()
    result = mixed[...]
    for c in range(chunks):
        arrive(*backs[c])
        back = unpack(order_v[2], came2[c])
        result = result + jnp.dot(
            back, wo[2 * c * LANES : 2 * (c + 1) * LANES, :], preferred_element_type=jnp.float32
        )
    out[...] = result.astype(jnp.bfloat16)


def local(lats, lons, expanded, stream, land, polar, land_shift, dw_kernel, w_proj, w_qkv, w_out, rel_bias):
    rows, cols, width_exp = expanded.shape
    width = stream.shape[2]
    heads = rel_bias.shape[0]
    count = rows * cols
    team = lats * GRID
    assert rows * lats == GRID * lats and count == LANES and GRID * (2 * GRID - 1) <= LANES
    table = jnp.transpose(rel_bias, (1, 2, 0)).reshape(-1, heads)
    home, away = orders(rows, cols, lats)
    rim_picks, spread, rim_home, inner_home = rim_tables(rows, cols, home)
    rim_count = len(rim_picks)
    assert cols & (cols - 1) == 0 and width_exp % (6 * LANES) == 0
    bf16, f32 = jnp.bfloat16, jnp.float32
    slabs = (team, 2 * count // team, width // 2)
    chunks = width // (2 * LANES)
    pieces = (chunks, team, 2 * count // team, LANES)
    any_ = pl.BlockSpec(memory_space=pl.ANY)
    vmem = pl.BlockSpec(memory_space=pltpu.VMEM)
    dma = pltpu.SemaphoreType.DMA
    result = pl.pallas_call(
        functools.partial(kernel, lats, lons, heads),
        out_shape=pltpu.VMEM((count, width), bf16),
        in_specs=[any_] * 18,
        out_specs=vmem,
        scratch_shapes=[
            pltpu.VMEM((rows + 2, cols, width_exp), bf16),
            pltpu.VMEM((2, rows, width_exp), bf16),
            pltpu.VMEM((4, 1, width_exp), f32),
            pltpu.VMEM((2, rows, width_exp), bf16),
            pltpu.VMEM((4, 1, width_exp), f32),
            pltpu.VMEM((count, width), bf16),
            pltpu.VMEM(w_proj.shape, bf16),
            pltpu.VMEM(w_qkv.shape, bf16),
            pltpu.VMEM(w_out.shape, bf16),
            pltpu.VMEM((4, rows, width_exp), f32),
            pltpu.VMEM((2, cols, width_exp), f32),
            pltpu.VMEM((2, rows, width_exp), f32),
            pltpu.VMEM((count - 2 * cols, width_exp), bf16),
            pltpu.VMEM((rim_count, width_exp), bf16),
            pltpu.VMEM((rim_count, width), f32),
            pltpu.VMEM((2 * count, width // 2), f32),
            pltpu.VMEM(slabs, bf16),
            pltpu.VMEM((rows, cols, LANES), f32),
            pltpu.VMEM((LANES, LANES), f32),
            pltpu.VMEM((count, width), f32),
            pltpu.VMEM((heads, GRID, LANES), f32),
            pltpu.VMEM((heads, GRID * GRID, LANES), f32),
            pltpu.VMEM((count, 3 * width), bf16),
            pltpu.VMEM(slabs, bf16),
            pltpu.VMEM(slabs, bf16),
            pltpu.VMEM(pieces, bf16),
            pltpu.VMEM(pieces, bf16),
            pltpu.VMEM((3,) + home.shape, bf16),
            pltpu.VMEM(inner_home.shape, bf16),
            pltpu.VMEM(rim_home.shape, bf16),
            pltpu.VMEM(rim_picks.shape, bf16),
            pltpu.VMEM(spread.shape, bf16),
            pltpu.SMEM(polar.shape, jnp.int32),
            pltpu.VMEM(land.shape, jnp.int32),
            pltpu.VMEM((1, width_exp), f32),
            pltpu.VMEM(dw_kernel.shape, f32),
            pltpu.VMEM(table.shape, f32),
            pltpu.VMEM((10 * 8, count), bf16),
            dma((18,)),
            dma((8,)),
            dma((8,)),
            dma,
            dma,
            dma((chunks,)),
            dma((chunks,)),
            dma((1 + chunks,)),
        ],
        compiler_params=pltpu.CompilerParams(collective_id=0, has_side_effects=True),
        name="section",
    )(
        expanded,
        stream.reshape(count, width),
        w_proj,
        w_qkv,
        w_out,
        polar,
        land,
        land_shift[None],
        dw_kernel,
        table,
        jnp.asarray(edge_picks(rows, cols), bf16),
        jnp.asarray(inner_home, bf16),
        jnp.asarray(rim_home, bf16),
        jnp.asarray(home.T, bf16),
        jnp.asarray(away, bf16),
        jnp.asarray(away.T, bf16),
        jnp.asarray(rim_picks, bf16),
        jnp.asarray(spread, bf16),
    )
    return result.reshape(rows, cols, width)


def solution(mesh):
    in_specs = (P("lat", "lon", None),) * 2 + (P("lat", "lon"),) + (P(),) * 7
    out_specs = P("lat", "lon", None)
    body = functools.partial(local, mesh.shape["lat"], mesh.shape["lon"])
    return jax.shard_map(body, mesh=mesh, in_specs=in_specs, out_specs=out_specs, check_vma=False)
```

```python
import functools

import jax
import jax.numpy as jnp
import numpy as np
from jax import lax
from jax.experimental import pallas as pl
from jax.experimental.pallas import tpu as pltpu
from jax.sharding import PartitionSpec as P

GRID = 8
LANES = 128
NEVER = -1e30

eps = 1e-05


def orders(rows, cols, lats):
    halves = GRID // lats
    packs = cols // GRID
    per = halves * packs
    count = rows * cols
    home = np.zeros((2 * count, 2 * count), np.float32)
    away = np.zeros((2 * count, 2 * count), np.float32)
    for lat in range(lats):
        for n in range(GRID):
            for a in range(halves):
                for g in range(packs):
                    for part in range(2):
                        slot = (lat * GRID + n) * 2 * per + part * per + a * packs + g
                        own = (a * lats + lat) * cols + g * GRID + n
                        group = (g * GRID + lat * halves + a) * GRID + n
                        home[slot, part * count + own] = 1
                        away[slot, part * count + group] = 1
    return home, away


def rim(rows, cols):
    west = [r * cols for r in range(rows)]
    east = [r * cols + cols - 1 for r in range(rows)]
    first = list(range(cols))
    last = list(range((rows - 1) * cols, rows * cols))
    return west + east + first + last


def rim_tables(rows, cols, home):
    count = rows * cols
    tokens = rim(rows, cols)
    picks = np.zeros((len(tokens), count), np.float32)
    spread = np.zeros((count, len(tokens)), np.float32)
    rim_home = np.zeros((2 * count, 2 * len(tokens)), np.float32)
    inner_home = home.copy()
    for at, token in enumerate(tokens):
        picks[at, token] = 1
        if tokens.index(token) == at:
            spread[token, at] = 1
            for part in range(2):
                rim_home[:, part * len(tokens) + at] = home[:, part * count + token]
                inner_home[:, part * count + token] = 0
    keep = [part * count + t for part in range(2) for t in range(cols, count - cols)]
    return picks, spread, rim_home, inner_home[:, keep]


def edge_picks(rows, cols):
    picks = np.zeros((10 * 8, rows * cols), np.float32)
    for r in range(rows):
        for at, c in ((0, 0), (1, cols - 1), (6, 0), (7, 1), (8, cols - 2), (9, cols - 1)):
            picks[8 * at + r, r * cols + c] = 1
    picks[16, 0] = 1
    picks[24, cols - 1] = 1
    picks[32, (rows - 1) * cols] = 1
    picks[40, rows * cols - 1] = 1
    return picks


def kernel(
    lats,
    lons,
    heads,
    expanded,
    stream,
    w_proj,
    w_qkv,
    w_out,
    polar_in,
    land_in,
    shift_in,
    taps_in,
    table_in,
    picks_in,
    inner_home_in,
    rim_home_in,
    home_t_in,
    away_in,
    away_t_in,
    rim_picks_in,
    spread_in,
    out,
    ext,
    edges,
    corners,
    side,
    corner_in,
    stream_v,
    wp,
    wq,
    wo,
    own_cols,
    partial,
    column_partial,
    active,
    rim_active,
    rim_total,
    slabs,
    early,
    lands,
    grid_table,
    mixed,
    turned,
    bias,
    qkv,
    sent1,
    came1,
    sent2,
    came2,
    order_v,
    inner_home,
    rim_home,
    rim_picks,
    spread,
    polar,
    land,
    shift,
    taps,
    table,
    picks,
    local_sem,
    halo_send,
    halo_recv,
    send1,
    recv1,
    send2,
    recv2,
    own_sem,
):
    rows, cols, width_exp = expanded.shape
    width = stream.shape[1]
    half = width // 2
    count = rows * cols
    team = lats * GRID
    stride = lons // GRID
    strip = lats
    members = GRID * GRID
    packs = count // members
    head_dim = width // heads
    lat = lax.axis_index("lat")
    lon = lax.axis_index("lon")
    member = lon // stride
    spot = lon % stride
    me = lat * GRID + member

    north, south = lax.rem(lat + lats - 1, lats), lax.rem(lat + 1, lats)
    west, east = lax.rem(lon + lons - 1, lons), lax.rem(lon + 1, lons)
    hops = [
        (i, j)
        for j in range(GRID)
        for i in sorted(range(lats), key=lambda i: -min(i, lats - i))
    ]

    def ahead(at, by, length):
        to = at + by
        return jnp.where(to >= length, to - length, to)

    def reach(i, j):
        far = jnp.where(member < GRID // 2, GRID - 1 - j, j)
        return ahead(lat, i, lats), far + (member % 2) * (1 - 2 * (far % 2))

    def is_other(to_lat, to_member):
        return (to_lat != lat) | (to_member != member)

    loads = [
        pltpu.make_async_copy(expanded, ext.at[pl.ds(1, rows)], local_sem.at[0]),
        pltpu.make_async_copy(stream, stream_v, local_sem.at[1]),
        pltpu.make_async_copy(w_proj, wp, local_sem.at[2]),
        pltpu.make_async_copy(w_qkv, wq, local_sem.at[3]),
        pltpu.make_async_copy(w_out, wo, local_sem.at[4]),
    ]
    for k, order in enumerate((away_t_in, away_in, home_t_in)):
        loads.append(pltpu.make_async_copy(order, order_v.at[k], local_sem.at[5 + k]))
    small = [
        pltpu.make_async_copy(src, dst, local_sem.at[8 + k])
        for k, (src, dst) in enumerate(
            [
                (picks_in, picks),
                (taps_in, taps),
                (shift_in, shift),
                (land_in, land),
                (table_in, table),
                (polar_in, polar),
                (inner_home_in, inner_home),
                (rim_home_in, rim_home),
                (rim_picks_in, rim_picks),
                (spread_in, spread),
            ]
        )
    ]
    for load in [loads[0]] + small[:4]:
        load.start()

    barrier = pltpu.get_barrier_semaphore()
    for i, j in hops:
        to_lat, to_member = reach(i, j)

        @pl.when(is_other(to_lat, to_member))
        def _():
            pl.semaphore_signal(
                barrier, inc=1, device_id={"lat": to_lat, "lon": to_member * stride + spot}
            )

    greeted = team - 1
    if stride > 1:
        for i in (north, lat, south):
            for j in (west, east):
                pl.semaphore_signal(barrier, inc=1, device_id={"lat": i, "lon": j})
        greeted += 6


    loads[0].wait()
    small[0].wait()
    for load in loads[2:3] + loads[1:2] + small[4:] + loads[3:]:
        load.start()
    block = ext[1 : rows + 1].reshape(count, width_exp)
    picked = jnp.dot(picks[0:48], block, preferred_element_type=jnp.float32)
    edges[0] = picked[0:rows].astype(jnp.bfloat16)
    edges[1] = picked[8 : 8 + rows].astype(jnp.bfloat16)
    for c in range(4):
        corners[c] = picked[16 + 8 * c : 17 + 8 * c]
    pl.semaphore_wait(barrier, greeted)

    def halo(src, dst, k, i, j):
        return pltpu.make_async_remote_copy(
            src_ref=src,
            dst_ref=dst,
            send_sem=halo_send.at[k],
            recv_sem=halo_recv.at[k],
            device_id={"lat": i, "lon": j},
        )

    side_halos = [
        halo(edges.at[1], side.at[0], 2, lat, east),
        halo(edges.at[0], side.at[1], 3, lat, west),
    ]
    south_halos = [
        halo(corners.at[3], corner_in.at[0], 4, south, east),
        halo(corners.at[2], corner_in.at[1], 5, south, west),
        halo(expanded.at[rows - 1], ext.at[0], 0, south, lon),
    ]
    north_halos = [
        halo(corners.at[1], corner_in.at[2], 6, north, east),
        halo(corners.at[0], corner_in.at[3], 7, north, west),
        halo(expanded.at[0], ext.at[rows + 1], 1, north, lon),
    ]
    for copy in side_halos:
        copy.start()

    @pl.when(lat < lats - 1)
    def _():
        for copy in south_halos:
            copy.start()

    @pl.when(lat > 0)
    def _():
        for copy in north_halos:
            copy.start()

    @pl.when(lat == 0)
    def _():
        ext[0] = jnp.zeros_like(ext[0])
        corner_in[0:2] = jnp.zeros_like(corner_in[0:2])

    @pl.when(lat == lats - 1)
    def _():
        ext[rows + 1] = jnp.zeros_like(ext[0])
        corner_in[2:4] = jnp.zeros_like(corner_in[0:2])

    picked = jnp.dot(picks[48:80], block, preferred_element_type=jnp.float32)
    for c in range(4):
        own_cols[c] = picked[8 * c : 8 * c + rows]
    for load in small[1:4]:
        load.wait()
    pick = lax.broadcasted_iota(jnp.int32, (cols, cols), 0)
    eye = (pick == lax.broadcasted_iota(jnp.int32, (cols, cols), 1)).astype(jnp.bfloat16)
    land_t = lax.dot_general(
        eye,
        land[...].astype(jnp.float32).astype(jnp.bfloat16),
        (((1,), (1,)), ((), ())),
        preferred_element_type=jnp.float32,
    )
    for r in range(rows):
        lands[r] = jnp.broadcast_to(land_t[:, r : r + 1], (cols, LANES))
    token = lax.broadcasted_iota(jnp.int32, (cols, LANES), 0)
    row_of = lax.broadcasted_iota(jnp.int32, (rows, LANES), 0)
    land_f = land[...].astype(jnp.float32)
    land_sides = [
        jnp.broadcast_to(land_f[:, c : c + 1], (rows, LANES)) for c in (0, cols - 1)
    ]

    def beside(x):
        before = jnp.where(token == 0, 0.0, pltpu.roll(x, 1, axis=0))
        after = jnp.where(token == cols - 1, 0.0, pltpu.roll(x, cols - 1, axis=0))
        return before, x, after

    def filter_own(c, _):
        at = pl.ds(pl.multiple_of(c * LANES, LANES), LANES)
        kern = [[taps[a, b : b + 1, at] for b in range(3)] for a in range(3)]
        shift_row = shift[:, at]
        near = {}
        for e in range(1, rows + 2):
            if e <= rows:
                near[e] = beside(ext[e, :, at].astype(jnp.float32))
            r = e - 2
            if r < 0:
                continue
            total_r = lands[r] * shift_row
            for a in range(3):
                if r + a in near:
                    for b in range(3):
                        total_r = total_r + near[r + a][b] * kern[a][b]
            if r == 0 or r == rows - 1:
                partial[0 if r == 0 else 1, :, at] = total_r
            else:
                active[(r - 1) * cols : r * cols, at] = jax.nn.gelu(total_r).astype(jnp.bfloat16)
        for k, (mid, other, b) in enumerate(((0, 1, 2), (3, 2, 0))):
            total_k = land_sides[k] * shift_row
            for at_col, tap in ((mid, 1), (other, b)):
                x = own_cols[at_col, :, at]
                up = jnp.where(row_of == 0, 0.0, pltpu.roll(x, 1, axis=0))
                down = jnp.where(row_of == rows - 1, 0.0, pltpu.roll(x, rows - 1, axis=0))
                total_k = total_k + up * kern[0][tap] + x * kern[1][tap] + down * kern[2][tap]
            column_partial[k, :, at] = total_k
        return 0

    lax.fori_loop(0, width_exp // LANES, filter_own, 0)

    def as_slabs(x):
        return x.reshape(team, 2 * count // team, x.shape[1]).astype(jnp.bfloat16)

    def unpack(order_t, slabs):
        flat = slabs.astype(jnp.float32).reshape(2 * count, slabs.shape[2]).astype(jnp.bfloat16)
        stacked = jnp.dot(order_t, flat, preferred_element_type=jnp.float32)
        return jnp.concatenate([stacked[:count], stacked[count:]], axis=1).astype(jnp.bfloat16)

    def hand(src, dst, sends, recvs, to_lat, to_member):
        return pltpu.make_async_remote_copy(
            src_ref=src.at[to_lat * GRID + to_member],
            dst_ref=dst.at[me],
            send_sem=sends,
            recv_sem=recvs,
            device_id={"lat": to_lat, "lon": to_member * stride + spot},
        )

    def send_early(*refs):
        for i, j in hops:
            to_lat, to_member = reach(i, j)
            copy = hand(*refs, to_lat, to_member)

            @pl.when(is_inner(to_lat, to_member) & is_other(to_lat, to_member))
            def _():
                copy.start()

    def is_inner(to_lat, to_member):
        return (to_lat > 0) & (to_lat < lats - 1) & (to_member > 0) & (to_member < GRID - 1)

    def is_head(to_lat, to_member):
        return (to_lat < 2) & (to_member == 0)

    def send_heads(*refs):
        for head in range(min(2, lats)):
            copy = hand(*refs, head, 0)

            @pl.when((lat != head) | (member != 0))
            def _():
                copy.start()

    def send_late(*refs):
        for i, j in hops:
            to_lat, to_member = reach(i, j)
            copy = hand(*refs, to_lat, to_member)
            skip = is_inner(to_lat, to_member)

            @pl.when(jnp.logical_not(skip) & is_other(to_lat, to_member))
            def _():
                copy.start()


    def send_back(*refs):
        send_heads(*refs)
        for i, j in hops:
            to_lat, to_member = reach(i, j)
            copy = hand(*refs, to_lat, to_member)

            @pl.when(jnp.logical_not(is_head(to_lat, to_member)) & is_other(to_lat, to_member))
            def _():
                copy.start()

    def arrive(src, dst, sends, recvs, own):
        pltpu.make_async_copy(src.at[me], dst.at[me], own).wait()
        others = pl.ds(0, team - 1)
        pltpu.make_async_copy(dst.at[others], dst.at[others], recvs).wait()
        pltpu.make_async_copy(src.at[others], src.at[others], sends).wait()

    loads[2].wait()
    loads[1].wait()
    for load in small[4:]:
        load.wait()

    def mix(base, projected):
        whole = (base + projected).astype(jnp.bfloat16)
        wide = whole.astype(jnp.float32)
        centred = wide - jnp.mean(wide, axis=1, keepdims=True)
        var = jnp.mean(centred * centred, axis=1, keepdims=True)
        normed = (centred * lax.rsqrt(var + eps)).astype(jnp.bfloat16)
        return whole, jnp.concatenate([normed[:, :half], normed[:, half:]], axis=0)

    inner_base = stream_v[cols : count - cols].astype(jnp.float32)
    inner_mixed, inner_stacked = mix(
        inner_base, jnp.dot(active[...], wp[...], preferred_element_type=jnp.float32)
    )
    mixed[cols : count - cols] = inner_mixed.astype(jnp.float32)
    slabs[...] = jnp.dot(inner_home[...], inner_stacked, preferred_element_type=jnp.float32)
    early[...] = as_slabs(slabs[...])
    send_early(early, came1, send1, recv1)
    rim_base = jnp.dot(rim_picks[...], stream_v[...], preferred_element_type=jnp.float32)

    for copy in side_halos:
        copy.wait()

    @pl.when(lat < lats - 1)
    def _():
        for copy in south_halos:
            copy.wait_send()
        for copy in north_halos:
            copy.wait_recv()

    @pl.when(lat > 0)
    def _():
        for copy in north_halos:
            copy.wait_send()
        for copy in south_halos:
            copy.wait_recv()

    def column(k, at, kern, b):
        x = side[k, :, at].astype(jnp.float32)
        above = corner_in[k, :, at]
        below = corner_in[2 + k, :, at]
        up = jnp.where(row_of == 0, above, pltpu.roll(x, 1, axis=0))
        down = jnp.where(row_of == rows - 1, below, pltpu.roll(x, rows - 1, axis=0))
        return up * kern[0][b] + x * kern[1][b] + down * kern[2][b]

    def filter_rim(start):
        at = pl.ds(pl.multiple_of(start, LANES), LANES)
        kern = [[taps[a, b : b + 1, at] for b in range(3)] for a in range(3)]
        sums = [column_partial[k, :, at] + column(k, at, kern, 2 * k) for k in range(2)]
        for k, (e, a, row) in enumerate(((0, 0, 0), (rows + 1, 2, rows - 1))):
            x = ext[e, :, at].astype(jnp.float32)
            far = beside(x)
            total_r = partial[k, :, at]
            for b in range(3):
                total_r = total_r + far[b] * kern[a][b]
            sums.append(total_r)
            west_far = x[0:1] * kern[a][1] + x[1:2] * kern[a][2]
            east_far = x[cols - 2 : cols - 1] * kern[a][0] + x[cols - 1 : cols] * kern[a][1]
            sums[0] = sums[0] + jnp.where(row_of == row, west_far, 0.0)
            sums[1] = sums[1] + jnp.where(row_of == row, east_far, 0.0)
        rim_active[:, at] = jax.nn.gelu(jnp.concatenate(sums, axis=0)).astype(jnp.bfloat16)

    steps = 6
    span = width_exp // steps

    def rim_term(c):
        at = pl.ds(pl.multiple_of(c * span, span), span)
        return jnp.dot(rim_active[:, at], wp[at, :], preferred_element_type=jnp.float32)

    def filter_span(c):
        for k in range(span // LANES):
            filter_rim(c * span + k * LANES)

    filter_span(0)
    rim_total[...] = jnp.zeros_like(rim_total)

    def rim_step(c, _):
        rim_total[...] = rim_total[...] + rim_term(c)
        filter_span(c + 1)
        return 0

    lax.fori_loop(0, steps - 1, rim_step, 0)
    rim_mixed, rim_stacked = mix(rim_base, rim_total[...] + rim_term(steps - 1))

    def spread_bias():
        lane = lax.broadcasted_iota(jnp.int32, (heads, LANES), 1)
        grid_table[...] = jnp.zeros_like(grid_table)
        for a in range(2 * GRID - 1):
            for b in range(GRID):
                to = (2 * GRID - 2 - a) * GRID + (GRID - b) % GRID
                grid_table[to : to + 1, :heads] = table[a * GRID + b : a * GRID + b + 1]
        flat = grid_table[...].T[:heads]
        for n in range(GRID):
            near = flat if n == 0 else pltpu.roll(flat, n, axis=1)
            far = pltpu.roll(flat, LANES - GRID + n, axis=1)
            turned[:, n, :] = jnp.where((lane & (GRID - 1)) >= n, near, far)
        lane8 = lax.broadcasted_iota(jnp.int32, (GRID, LANES), 1)
        open_key = [
            jnp.full((GRID, LANES), polar[m * strip + lat], jnp.int32) == 0 for m in range(GRID)
        ]

        def fill(h, _):
            own = turned[h]
            for m in range(GRID):
                moved = None
                for g in range(packs):
                    by = (g * members + LANES - (GRID - 1 - m) * GRID) % LANES
                    here = own if by == 0 else pltpu.roll(own, by, axis=1)
                    moved = here if g == 0 else jnp.where(lane8 >= g * members, here, moved)
                bias[h, m * GRID : (m + 1) * GRID, :] = jnp.where(open_key[m], moved, NEVER)
            return 0

        lax.fori_loop(0, heads, fill, 0)

    for load in loads[5:]:
        load.wait()
    sent1[...] = as_slabs(
        slabs[...] + jnp.dot(rim_home[...], rim_stacked, preferred_element_type=jnp.float32)
    )
    first = (sent1, came1, send1, recv1, own_sem.at[0])
    pltpu.make_async_copy(sent1.at[me], came1.at[me], own_sem.at[0]).start()
    send_late(sent1, came1, send1, recv1)
    spread_bias()
    fixed = jnp.dot(spread[...], rim_mixed, preferred_element_type=jnp.float32)
    mixed[0:cols] = fixed[0:cols]
    mixed[count - cols : count] = fixed[count - cols : count]
    column_of = lax.broadcasted_iota(jnp.int32, (count - 2 * cols, width), 0) & (cols - 1)
    mixed[cols : count - cols] = jnp.where(
        (column_of == 0) | (column_of == cols - 1),
        fixed[cols : count - cols],
        mixed[cols : count - cols],
    )
    loads[3].wait()
    arrive(*first)
    tokens = unpack(order_v[0], came1[...])

    per = LANES // head_dim
    lane_head = lax.broadcasted_iota(jnp.int32, (count, LANES), 1) // head_dim
    query_lane = lax.broadcasted_iota(jnp.int32, (members, LANES), 1) // members
    ones = jnp.ones((16, LANES), jnp.bfloat16)
    scale = head_dim ** (-0.5)

    none = jnp.zeros((members, LANES), jnp.bfloat16)

    def score(p):
        q, k = (
            qkv[:, part * width + p * LANES : part * width + (p + 1) * LANES] for part in range(2)
        )
        keys = jnp.concatenate([k[g * members : (g + 1) * members] for g in range(packs)], axis=1)
        zero = jnp.zeros_like(q)
        queries = []
        for h in range(per):
            own = jnp.where(lane_head == h, q, zero)
            for g in range(packs):
                part = own[g * members : (g + 1) * members]
                queries.append(
                    jnp.concatenate([part if f == g else none for f in range(packs)], axis=1)
                )
        return lax.dot_general(
            keys,
            jnp.concatenate(queries, axis=0),
            (((1,), (1,)), ((), ())),
            preferred_element_type=jnp.float32,
        )

    def soften(p, scores_all):
        spread_all = []
        for h in range(per):
            scores = scores_all[:, h * count : (h + 1) * count] * scale + bias[p * per + h]
            weights = jnp.exp(scores - jnp.max(scores, axis=0, keepdims=True))
            weights = weights.astype(jnp.bfloat16)
            spread_all.append(
                jnp.concatenate(
                    [jnp.where(query_lane == g, weights, none) for g in range(packs)], axis=0
                )
            )
        return spread_all

    def gather(p, spread_all):
        v_t = qkv[:, 2 * width + p * LANES : 2 * width + (p + 1) * LANES].T
        summed = [
            jnp.dot(
                jnp.concatenate([v_t[h * head_dim : (h + 2) * head_dim], ones], axis=0),
                jnp.concatenate(spread_all[h : h + 2], axis=1),
                preferred_element_type=jnp.float32,
            )
            for h in range(0, per, 2)
        ]
        done = []
        for h in range(per):
            e = h % 2
            mine = summed[h // 2][:, e * count : (e + 1) * count]
            total_h = mine[2 * head_dim : 2 * head_dim + 1]
            done.append(mine[e * head_dim : (e + 1) * head_dim] * (1.0 / total_h))
        return jnp.concatenate(done, axis=0).astype(jnp.bfloat16)

    def attend_pair(c):
        pair = (2 * c, 2 * c + 1)
        scored = [score(p) for p in pair]
        softened = [soften(p, x) for p, x in zip(pair, scored)]
        return [gather(p, x) for p, x in zip(pair, softened)]

    chunks = width // (2 * LANES)
    backs = [
        (sent2.at[c], came2.at[c], send2.at[c], recv2.at[c], own_sem.at[1 + c])
        for c in range(chunks)
    ]
    for c in range(chunks):
        for part in range(3):
            at = part * width + 2 * c * LANES
            qkv[:, at : at + 2 * LANES] = jnp.dot(
                tokens, wq[:, at : at + 2 * LANES], preferred_element_type=jnp.float32
            ).astype(jnp.bfloat16)
        pair = jnp.concatenate(attend_pair(c), axis=1)
        sent2[c] = as_slabs(
            lax.dot_general(
                order_v[1], pair, (((1,), (1,)), ((), ())), preferred_element_type=jnp.float32
            )
        )
        pltpu.make_async_copy(sent2.at[c, me], came2.at[c, me], own_sem.at[1 + c]).start()
        send_back(*backs[c][:4])

    loads[4].wait()
    result = mixed[...]
    for c in range(chunks):
        arrive(*backs[c])
        back = unpack(order_v[2], came2[c])
        result = result + jnp.dot(
            back, wo[2 * c * LANES : 2 * (c + 1) * LANES, :], preferred_element_type=jnp.float32
        )
    out[...] = result.astype(jnp.bfloat16)


def local(lats, lons, expanded, stream, land, polar, land_shift, dw_kernel, w_proj, w_qkv, w_out, rel_bias):
    rows, cols, width_exp = expanded.shape
    width = stream.shape[2]
    heads = rel_bias.shape[0]
    count = rows * cols
    team = lats * GRID
    assert rows * lats == GRID * lats and count == LANES and GRID * (2 * GRID - 1) <= LANES
    table = jnp.transpose(rel_bias, (1, 2, 0)).reshape(-1, heads)
    home, away = orders(rows, cols, lats)
    rim_picks, spread, rim_home, inner_home = rim_tables(rows, cols, home)
    rim_count = len(rim_picks)
    assert cols & (cols - 1) == 0 and width_exp % (6 * LANES) == 0
    bf16, f32 = jnp.bfloat16, jnp.float32
    slabs = (team, 2 * count // team, width // 2)
    chunks = width // (2 * LANES)
    pieces = (chunks, team, 2 * count // team, LANES)
    any_ = pl.BlockSpec(memory_space=pl.ANY)
    vmem = pl.BlockSpec(memory_space=pltpu.VMEM)
    dma = pltpu.SemaphoreType.DMA
    result = pl.pallas_call(
        functools.partial(kernel, lats, lons, heads),
        out_shape=pltpu.VMEM((count, width), bf16),
        in_specs=[any_] * 18,
        out_specs=vmem,
        scratch_shapes=[
            pltpu.VMEM((rows + 2, cols, width_exp), bf16),
            pltpu.VMEM((2, rows, width_exp), bf16),
            pltpu.VMEM((4, 1, width_exp), f32),
            pltpu.VMEM((2, rows, width_exp), bf16),
            pltpu.VMEM((4, 1, width_exp), f32),
            pltpu.VMEM((count, width), bf16),
            pltpu.VMEM(w_proj.shape, bf16),
            pltpu.VMEM(w_qkv.shape, bf16),
            pltpu.VMEM(w_out.shape, bf16),
            pltpu.VMEM((4, rows, width_exp), f32),
            pltpu.VMEM((2, cols, width_exp), f32),
            pltpu.VMEM((2, rows, width_exp), f32),
            pltpu.VMEM((count - 2 * cols, width_exp), bf16),
            pltpu.VMEM((rim_count, width_exp), bf16),
            pltpu.VMEM((rim_count, width), f32),
            pltpu.VMEM((2 * count, width // 2), f32),
            pltpu.VMEM(slabs, bf16),
            pltpu.VMEM((rows, cols, LANES), f32),
            pltpu.VMEM((LANES, LANES), f32),
            pltpu.VMEM((count, width), f32),
            pltpu.VMEM((heads, GRID, LANES), f32),
            pltpu.VMEM((heads, GRID * GRID, LANES), f32),
            pltpu.VMEM((count, 3 * width), bf16),
            pltpu.VMEM(slabs, bf16),
            pltpu.VMEM(slabs, bf16),
            pltpu.VMEM(pieces, bf16),
            pltpu.VMEM(pieces, bf16),
            pltpu.VMEM((3,) + home.shape, bf16),
            pltpu.VMEM(inner_home.shape, bf16),
            pltpu.VMEM(rim_home.shape, bf16),
            pltpu.VMEM(rim_picks.shape, bf16),
            pltpu.VMEM(spread.shape, bf16),
            pltpu.SMEM(polar.shape, jnp.int32),
            pltpu.VMEM(land.shape, jnp.int32),
            pltpu.VMEM((1, width_exp), f32),
            pltpu.VMEM(dw_kernel.shape, f32),
            pltpu.VMEM(table.shape, f32),
            pltpu.VMEM((10 * 8, count), bf16),
            dma((18,)),
            dma((8,)),
            dma((8,)),
            dma,
            dma,
            dma((chunks,)),
            dma((chunks,)),
            dma((1 + chunks,)),
        ],
        compiler_params=pltpu.CompilerParams(collective_id=0, has_side_effects=True),
        name="section",
    )(
        expanded,
        stream.reshape(count, width),
        w_proj,
        w_qkv,
        w_out,
        polar,
        land,
        land_shift[None],
        dw_kernel,
        table,
        jnp.asarray(edge_picks(rows, cols), bf16),
        jnp.asarray(inner_home, bf16),
        jnp.asarray(rim_home, bf16),
        jnp.asarray(home.T, bf16),
        jnp.asarray(away, bf16),
        jnp.asarray(away.T, bf16),
        jnp.asarray(rim_picks, bf16),
        jnp.asarray(spread, bf16),
    )
    return result.reshape(rows, cols, width)


def solution(mesh):
    in_specs = (P("lat", "lon", None),) * 2 + (P("lat", "lon"),) + (P(),) * 7
    out_specs = P("lat", "lon", None)
    body = functools.partial(local, mesh.shape["lat"], mesh.shape["lon"])
    return jax.shard_map(body, mesh=mesh, in_specs=in_specs, out_specs=out_specs, check_vma=False)
```

```python
import functools

import jax
import jax.numpy as jnp
import numpy as np
from jax import lax
from jax.experimental import pallas as pl
from jax.experimental.pallas import tpu as pltpu
from jax.sharding import PartitionSpec as P

GRID = 8
LANES = 128
NEVER = -1e30

eps = 1e-05


def orders(rows, cols, lats):
    halves = GRID // lats
    packs = cols // GRID
    per = halves * packs
    count = rows * cols
    home = np.zeros((2 * count, 2 * count), np.float32)
    away = np.zeros((2 * count, 2 * count), np.float32)
    for lat in range(lats):
        for n in range(GRID):
            for a in range(halves):
                for g in range(packs):
                    for part in range(2):
                        slot = (lat * GRID + n) * 2 * per + part * per + a * packs + g
                        own = (a * lats + lat) * cols + g * GRID + n
                        group = (g * GRID + lat * halves + a) * GRID + n
                        home[slot, part * count + own] = 1
                        away[slot, part * count + group] = 1
    return home, away


def rim(rows, cols):
    west = [r * cols for r in range(rows)]
    east = [r * cols + cols - 1 for r in range(rows)]
    first = list(range(cols))
    last = list(range((rows - 1) * cols, rows * cols))
    return west + east + first + last


def rim_tables(rows, cols, home):
    count = rows * cols
    tokens = rim(rows, cols)
    picks = np.zeros((len(tokens), count), np.float32)
    spread = np.zeros((count, len(tokens)), np.float32)
    rim_home = np.zeros((2 * count, 2 * len(tokens)), np.float32)
    inner_home = home.copy()
    for at, token in enumerate(tokens):
        picks[at, token] = 1
        if tokens.index(token) == at:
            spread[token, at] = 1
            for part in range(2):
                rim_home[:, part * len(tokens) + at] = home[:, part * count + token]
                inner_home[:, part * count + token] = 0
    keep = [part * count + t for part in range(2) for t in range(cols, count - cols)]
    return picks, spread, rim_home, inner_home[:, keep]


def edge_picks(rows, cols):
    picks = np.zeros((10 * 8, rows * cols), np.float32)
    for r in range(rows):
        for at, c in ((0, 0), (1, cols - 1), (6, 0), (7, 1), (8, cols - 2), (9, cols - 1)):
            picks[8 * at + r, r * cols + c] = 1
    picks[16, 0] = 1
    picks[24, cols - 1] = 1
    picks[32, (rows - 1) * cols] = 1
    picks[40, rows * cols - 1] = 1
    return picks


def kernel(
    lats,
    lons,
    heads,
    expanded,
    stream,
    w_proj,
    w_qkv,
    w_out,
    polar_in,
    land_in,
    shift_in,
    taps_in,
    table_in,
    picks_in,
    inner_home_in,
    rim_home_in,
    home_t_in,
    away_in,
    away_t_in,
    rim_picks_in,
    spread_in,
    out,
    ext,
    edges,
    corners,
    side,
    corner_in,
    stream_v,
    wp,
    wq,
    wo,
    own_cols,
    partial,
    column_partial,
    active,
    rim_active,
    rim_total,
    slabs,
    early,
    lands,
    grid_table,
    mixed,
    turned,
    bias,
    qkv,
    sent1,
    came1,
    sent2,
    came2,
    order_v,
    inner_home,
    rim_home,
    rim_picks,
    spread,
    polar,
    land,
    shift,
    taps,
    table,
    picks,
    local_sem,
    halo_send,
    halo_recv,
    send1,
    recv1,
    send2,
    recv2,
    own_sem,
):
    rows, cols, width_exp = expanded.shape
    width = stream.shape[1]
    half = width // 2
    count = rows * cols
    team = lats * GRID
    stride = lons // GRID
    strip = lats
    members = GRID * GRID
    packs = count // members
    head_dim = width // heads
    lat = lax.axis_index("lat")
    lon = lax.axis_index("lon")
    member = lon // stride
    spot = lon % stride
    me = lat * GRID + member

    north, south = lax.rem(lat + lats - 1, lats), lax.rem(lat + 1, lats)
    west, east = lax.rem(lon + lons - 1, lons), lax.rem(lon + 1, lons)
    hops = [
        (i, j)
        for j in range(GRID)
        for i in sorted(range(lats), key=lambda i: -min(i, lats - i))
    ]

    def ahead(at, by, length):
        to = at + by
        return jnp.where(to >= length, to - length, to)

    def reach(i, j):
        far = jnp.where(member < GRID // 2, GRID - 1 - j, j)
        return ahead(lat, i, lats), far + (member % 2) * (1 - 2 * (far % 2))

    def is_other(to_lat, to_member):
        return (to_lat != lat) | (to_member != member)

    loads = [
        pltpu.make_async_copy(expanded, ext.at[pl.ds(1, rows)], local_sem.at[0]),
        pltpu.make_async_copy(stream, stream_v, local_sem.at[1]),
        pltpu.make_async_copy(w_proj, wp, local_sem.at[2]),
        pltpu.make_async_copy(w_qkv, wq, local_sem.at[3]),
        pltpu.make_async_copy(w_out, wo, local_sem.at[4]),
    ]
    for k, order in enumerate((away_t_in, away_in, home_t_in)):
        loads.append(pltpu.make_async_copy(order, order_v.at[k], local_sem.at[5 + k]))
    small = [
        pltpu.make_async_copy(src, dst, local_sem.at[8 + k])
        for k, (src, dst) in enumerate(
            [
                (picks_in, picks),
                (taps_in, taps),
                (shift_in, shift),
                (land_in, land),
                (table_in, table),
                (polar_in, polar),
                (inner_home_in, inner_home),
                (rim_home_in, rim_home),
                (rim_picks_in, rim_picks),
                (spread_in, spread),
            ]
        )
    ]
    for load in [loads[0]] + small[:4]:
        load.start()

    barrier = pltpu.get_barrier_semaphore()
    for i, j in hops:
        to_lat, to_member = reach(i, j)

        @pl.when(is_other(to_lat, to_member))
        def _():
            pl.semaphore_signal(
                barrier, inc=1, device_id={"lat": to_lat, "lon": to_member * stride + spot}
            )

    greeted = team - 1
    if stride > 1:
        for i in (north, lat, south):
            for j in (west, east):
                pl.semaphore_signal(barrier, inc=1, device_id={"lat": i, "lon": j})
        greeted += 6


    loads[0].wait()
    small[0].wait()
    for load in loads[2:3] + loads[1:2] + small[4:] + loads[3:]:
        load.start()
    block = ext[1 : rows + 1].reshape(count, width_exp)
    picked = jnp.dot(picks[0:48], block, preferred_element_type=jnp.float32)
    edges[0] = picked[0:rows].astype(jnp.bfloat16)
    edges[1] = picked[8 : 8 + rows].astype(jnp.bfloat16)
    for c in range(4):
        corners[c] = picked[16 + 8 * c : 17 + 8 * c]
    pl.semaphore_wait(barrier, greeted)

    def halo(src, dst, k, i, j):
        return pltpu.make_async_remote_copy(
            src_ref=src,
            dst_ref=dst,
            send_sem=halo_send.at[k],
            recv_sem=halo_recv.at[k],
            device_id={"lat": i, "lon": j},
        )

    side_halos = [
        halo(edges.at[1], side.at[0], 2, lat, east),
        halo(edges.at[0], side.at[1], 3, lat, west),
    ]
    south_halos = [
        halo(corners.at[3], corner_in.at[0], 4, south, east),
        halo(corners.at[2], corner_in.at[1], 5, south, west),
        halo(expanded.at[rows - 1], ext.at[0], 0, south, lon),
    ]
    north_halos = [
        halo(corners.at[1], corner_in.at[2], 6, north, east),
        halo(corners.at[0], corner_in.at[3], 7, north, west),
        halo(expanded.at[0], ext.at[rows + 1], 1, north, lon),
    ]
    for copy in side_halos:
        copy.start()

    @pl.when(lat < lats - 1)
    def _():
        for copy in south_halos:
            copy.start()

    @pl.when(lat > 0)
    def _():
        for copy in north_halos:
            copy.start()

    @pl.when(lat == 0)
    def _():
        ext[0] = jnp.zeros_like(ext[0])
        corner_in[0:2] = jnp.zeros_like(corner_in[0:2])

    @pl.when(lat == lats - 1)
    def _():
        ext[rows + 1] = jnp.zeros_like(ext[0])
        corner_in[2:4] = jnp.zeros_like(corner_in[0:2])

    picked = jnp.dot(picks[48:80], block, preferred_element_type=jnp.float32)
    for c in range(4):
        own_cols[c] = picked[8 * c : 8 * c + rows]
    for load in small[1:4]:
        load.wait()
    pick = lax.broadcasted_iota(jnp.int32, (cols, cols), 0)
    eye = (pick == lax.broadcasted_iota(jnp.int32, (cols, cols), 1)).astype(jnp.bfloat16)
    land_t = lax.dot_general(
        eye,
        land[...].astype(jnp.float32).astype(jnp.bfloat16),
        (((1,), (1,)), ((), ())),
        preferred_element_type=jnp.float32,
    )
    for r in range(rows):
        lands[r] = jnp.broadcast_to(land_t[:, r : r + 1], (cols, LANES))
    token = lax.broadcasted_iota(jnp.int32, (cols, LANES), 0)
    row_of = lax.broadcasted_iota(jnp.int32, (rows, LANES), 0)
    land_f = land[...].astype(jnp.float32)
    land_sides = [
        jnp.broadcast_to(land_f[:, c : c + 1], (rows, LANES)) for c in (0, cols - 1)
    ]

    def beside(x):
        before = jnp.where(token == 0, 0.0, pltpu.roll(x, 1, axis=0))
        after = jnp.where(token == cols - 1, 0.0, pltpu.roll(x, cols - 1, axis=0))
        return before, x, after

    def filter_own(c, _):
        at = pl.ds(pl.multiple_of(c * LANES, LANES), LANES)
        kern = [[taps[a, b : b + 1, at] for b in range(3)] for a in range(3)]
        shift_row = shift[:, at]
        near = {}
        for e in range(1, rows + 2):
            if e <= rows:
                near[e] = beside(ext[e, :, at].astype(jnp.float32))
            r = e - 2
            if r < 0:
                continue
            total_r = lands[r] * shift_row
            for a in range(3):
                if r + a in near:
                    for b in range(3):
                        total_r = total_r + near[r + a][b] * kern[a][b]
            if r == 0 or r == rows - 1:
                partial[0 if r == 0 else 1, :, at] = total_r
            else:
                active[(r - 1) * cols : r * cols, at] = jax.nn.gelu(total_r).astype(jnp.bfloat16)
        for k, (mid, other, b) in enumerate(((0, 1, 2), (3, 2, 0))):
            total_k = land_sides[k] * shift_row
            for at_col, tap in ((mid, 1), (other, b)):
                x = own_cols[at_col, :, at]
                up = jnp.where(row_of == 0, 0.0, pltpu.roll(x, 1, axis=0))
                down = jnp.where(row_of == rows - 1, 0.0, pltpu.roll(x, rows - 1, axis=0))
                total_k = total_k + up * kern[0][tap] + x * kern[1][tap] + down * kern[2][tap]
            column_partial[k, :, at] = total_k
        return 0

    lax.fori_loop(0, width_exp // LANES, filter_own, 0)

    def as_slabs(x):
        return x.reshape(team, 2 * count // team, x.shape[1]).astype(jnp.bfloat16)

    def unpack(order_t, slabs):
        flat = slabs.astype(jnp.float32).reshape(2 * count, slabs.shape[2]).astype(jnp.bfloat16)
        stacked = jnp.dot(order_t, flat, preferred_element_type=jnp.float32)
        return jnp.concatenate([stacked[:count], stacked[count:]], axis=1).astype(jnp.bfloat16)

    def hand(src, dst, sends, recvs, to_lat, to_member):
        return pltpu.make_async_remote_copy(
            src_ref=src.at[to_lat * GRID + to_member],
            dst_ref=dst.at[me],
            send_sem=sends,
            recv_sem=recvs,
            device_id={"lat": to_lat, "lon": to_member * stride + spot},
        )

    def send_early(*refs):
        for i, j in hops:
            to_lat, to_member = reach(i, j)
            copy = hand(*refs, to_lat, to_member)

            @pl.when(is_inner(to_lat, to_member) & is_other(to_lat, to_member))
            def _():
                copy.start()

    def is_inner(to_lat, to_member):
        return (to_lat > 0) & (to_lat < lats - 1) & (to_member > 0) & (to_member < GRID - 1)

    def is_head(to_lat, to_member):
        return (to_lat < 2) & (to_member == 0)

    def send_heads(*refs):
        for head in range(min(2, lats)):
            copy = hand(*refs, head, 0)

            @pl.when((lat != head) | (member != 0))
            def _():
                copy.start()

    def send_late(*refs):
        for i, j in hops:
            to_lat, to_member = reach(i, j)
            copy = hand(*refs, to_lat, to_member)
            skip = is_inner(to_lat, to_member)

            @pl.when(jnp.logical_not(skip) & is_other(to_lat, to_member))
            def _():
                copy.start()


    def send_back(*refs):
        send_heads(*refs)
        for i, j in hops:
            to_lat, to_member = reach(i, j)
            copy = hand(*refs, to_lat, to_member)

            @pl.when(jnp.logical_not(is_head(to_lat, to_member)) & is_other(to_lat, to_member))
            def _():
                copy.start()

    def arrive(src, dst, sends, recvs, own):
        pltpu.make_async_copy(src.at[me], dst.at[me], own).wait()
        others = pl.ds(0, team - 1)
        pltpu.make_async_copy(dst.at[others], dst.at[others], recvs).wait()
        pltpu.make_async_copy(src.at[others], src.at[others], sends).wait()

    loads[2].wait()
    loads[1].wait()
    for load in small[4:]:
        load.wait()

    def mix(base, projected):
        whole = (base + projected).astype(jnp.bfloat16)
        wide = whole.astype(jnp.float32)
        centred = wide - jnp.mean(wide, axis=1, keepdims=True)
        var = jnp.mean(centred * centred, axis=1, keepdims=True)
        normed = (centred * lax.rsqrt(var + eps)).astype(jnp.bfloat16)
        return whole, jnp.concatenate([normed[:, :half], normed[:, half:]], axis=0)

    inner_base = stream_v[cols : count - cols].astype(jnp.float32)
    inner_mixed, inner_stacked = mix(
        inner_base, jnp.dot(active[...], wp[...], preferred_element_type=jnp.float32)
    )
    mixed[cols : count - cols] = inner_mixed.astype(jnp.float32)
    slabs[...] = jnp.dot(inner_home[...], inner_stacked, preferred_element_type=jnp.float32)
    early[...] = as_slabs(slabs[...])
    send_early(early, came1, send1, recv1)
    rim_base = jnp.dot(rim_picks[...], stream_v[...], preferred_element_type=jnp.float32)

    for copy in side_halos:
        copy.wait()

    @pl.when(lat < lats - 1)
    def _():
        for copy in south_halos:
            copy.wait_send()
        for copy in north_halos:
            copy.wait_recv()

    @pl.when(lat > 0)
    def _():
        for copy in north_halos:
            copy.wait_send()
        for copy in south_halos:
            copy.wait_recv()

    def column(k, at, kern, b):
        x = side[k, :, at].astype(jnp.float32)
        above = corner_in[k, :, at]
        below = corner_in[2 + k, :, at]
        up = jnp.where(row_of == 0, above, pltpu.roll(x, 1, axis=0))
        down = jnp.where(row_of == rows - 1, below, pltpu.roll(x, rows - 1, axis=0))
        return up * kern[0][b] + x * kern[1][b] + down * kern[2][b]

    def filter_rim(start):
        at = pl.ds(pl.multiple_of(start, LANES), LANES)
        kern = [[taps[a, b : b + 1, at] for b in range(3)] for a in range(3)]
        sums = [column_partial[k, :, at] + column(k, at, kern, 2 * k) for k in range(2)]
        for k, (e, a, row) in enumerate(((0, 0, 0), (rows + 1, 2, rows - 1))):
            x = ext[e, :, at].astype(jnp.float32)
            far = beside(x)
            total_r = partial[k, :, at]
            for b in range(3):
                total_r = total_r + far[b] * kern[a][b]
            sums.append(total_r)
            west_far = x[0:1] * kern[a][1] + x[1:2] * kern[a][2]
            east_far = x[cols - 2 : cols - 1] * kern[a][0] + x[cols - 1 : cols] * kern[a][1]
            sums[0] = sums[0] + jnp.where(row_of == row, west_far, 0.0)
            sums[1] = sums[1] + jnp.where(row_of == row, east_far, 0.0)
        rim_active[:, at] = jax.nn.gelu(jnp.concatenate(sums, axis=0)).astype(jnp.bfloat16)

    steps = 3
    span = width_exp // steps

    def rim_term(c):
        at = pl.ds(pl.multiple_of(c * span, span), span)
        return jnp.dot(rim_active[:, at], wp[at, :], preferred_element_type=jnp.float32)

    def filter_span(c):
        for k in range(span // LANES):
            filter_rim(c * span + k * LANES)

    filter_span(0)
    rim_total[...] = jnp.zeros_like(rim_total)

    def rim_step(c, _):
        rim_total[...] = rim_total[...] + rim_term(c)
        filter_span(c + 1)
        return 0

    lax.fori_loop(0, steps - 1, rim_step, 0)
    rim_mixed, rim_stacked = mix(rim_base, rim_total[...] + rim_term(steps - 1))

    def spread_bias():
        lane = lax.broadcasted_iota(jnp.int32, (heads, LANES), 1)
        grid_table[...] = jnp.zeros_like(grid_table)
        for a in range(2 * GRID - 1):
            for b in range(GRID):
                to = (2 * GRID - 2 - a) * GRID + (GRID - b) % GRID
                grid_table[to : to + 1, :heads] = table[a * GRID + b : a * GRID + b + 1]
        flat = grid_table[...].T[:heads]
        for n in range(GRID):
            near = flat if n == 0 else pltpu.roll(flat, n, axis=1)
            far = pltpu.roll(flat, LANES - GRID + n, axis=1)
            turned[:, n, :] = jnp.where((lane & (GRID - 1)) >= n, near, far)
        lane8 = lax.broadcasted_iota(jnp.int32, (GRID, LANES), 1)
        open_key = [
            jnp.full((GRID, LANES), polar[m * strip + lat], jnp.int32) == 0 for m in range(GRID)
        ]

        def fill(h, _):
            own = turned[h]
            for m in range(GRID):
                moved = None
                for g in range(packs):
                    by = (g * members + LANES - (GRID - 1 - m) * GRID) % LANES
                    here = own if by == 0 else pltpu.roll(own, by, axis=1)
                    moved = here if g == 0 else jnp.where(lane8 >= g * members, here, moved)
                bias[h, m * GRID : (m + 1) * GRID, :] = jnp.where(open_key[m], moved, NEVER)
            return 0

        lax.fori_loop(0, heads, fill, 0)

    for load in loads[5:]:
        load.wait()
    sent1[...] = as_slabs(
        slabs[...] + jnp.dot(rim_home[...], rim_stacked, preferred_element_type=jnp.float32)
    )
    first = (sent1, came1, send1, recv1, own_sem.at[0])
    pltpu.make_async_copy(sent1.at[me], came1.at[me], own_sem.at[0]).start()
    send_late(sent1, came1, send1, recv1)
    spread_bias()
    fixed = jnp.dot(spread[...], rim_mixed, preferred_element_type=jnp.float32)
    mixed[0:cols] = fixed[0:cols]
    mixed[count - cols : count] = fixed[count - cols : count]
    column_of = lax.broadcasted_iota(jnp.int32, (count - 2 * cols, width), 0) & (cols - 1)
    mixed[cols : count - cols] = jnp.where(
        (column_of == 0) | (column_of == cols - 1),
        fixed[cols : count - cols],
        mixed[cols : count - cols],
    )
    loads[3].wait()
    arrive(*first)
    tokens = unpack(order_v[0], came1[...])

    per = LANES // head_dim
    lane_head = lax.broadcasted_iota(jnp.int32, (count, LANES), 1) // head_dim
    query_lane = lax.broadcasted_iota(jnp.int32, (members, LANES), 1) // members
    ones = jnp.ones((16, LANES), jnp.bfloat16)
    scale = head_dim ** (-0.5)

    none = jnp.zeros((members, LANES), jnp.bfloat16)

    def score(p):
        q, k = (
            qkv[:, part * width + p * LANES : part * width + (p + 1) * LANES] for part in range(2)
        )
        keys = jnp.concatenate([k[g * members : (g + 1) * members] for g in range(packs)], axis=1)
        zero = jnp.zeros_like(q)
        queries = []
        for h in range(per):
            own = jnp.where(lane_head == h, q, zero)
            for g in range(packs):
                part = own[g * members : (g + 1) * members]
                queries.append(
                    jnp.concatenate([part if f == g else none for f in range(packs)], axis=1)
                )
        return lax.dot_general(
            keys,
            jnp.concatenate(queries, axis=0),
            (((1,), (1,)), ((), ())),
            preferred_element_type=jnp.float32,
        )

    def soften(p, scores_all):
        spread_all = []
        for h in range(per):
            scores = scores_all[:, h * count : (h + 1) * count] * scale + bias[p * per + h]
            weights = jnp.exp(scores - jnp.max(scores, axis=0, keepdims=True))
            weights = weights.astype(jnp.bfloat16)
            spread_all.append(
                jnp.concatenate(
                    [jnp.where(query_lane == g, weights, none) for g in range(packs)], axis=0
                )
            )
        return spread_all

    def gather(p, spread_all):
        v_t = qkv[:, 2 * width + p * LANES : 2 * width + (p + 1) * LANES].T
        summed = [
            jnp.dot(
                jnp.concatenate([v_t[h * head_dim : (h + 2) * head_dim], ones], axis=0),
                jnp.concatenate(spread_all[h : h + 2], axis=1),
                preferred_element_type=jnp.float32,
            )
            for h in range(0, per, 2)
        ]
        done = []
        for h in range(per):
            e = h % 2
            mine = summed[h // 2][:, e * count : (e + 1) * count]
            total_h = mine[2 * head_dim : 2 * head_dim + 1]
            done.append(mine[e * head_dim : (e + 1) * head_dim] * (1.0 / total_h))
        return jnp.concatenate(done, axis=0).astype(jnp.bfloat16)

    def attend_pair(c):
        pair = (2 * c, 2 * c + 1)
        scored = [score(p) for p in pair]
        softened = [soften(p, x) for p, x in zip(pair, scored)]
        return [gather(p, x) for p, x in zip(pair, softened)]

    chunks = width // (2 * LANES)
    backs = [
        (sent2.at[c], came2.at[c], send2.at[c], recv2.at[c], own_sem.at[1 + c])
        for c in range(chunks)
    ]
    for c in range(chunks):
        for part in range(3):
            at = part * width + 2 * c * LANES
            qkv[:, at : at + 2 * LANES] = jnp.dot(
                tokens, wq[:, at : at + 2 * LANES], preferred_element_type=jnp.float32
            ).astype(jnp.bfloat16)
        pair = jnp.concatenate(attend_pair(c), axis=1)
        sent2[c] = as_slabs(
            lax.dot_general(
                order_v[1], pair, (((1,), (1,)), ((), ())), preferred_element_type=jnp.float32
            )
        )
        pltpu.make_async_copy(sent2.at[c, me], came2.at[c, me], own_sem.at[1 + c]).start()
        send_back(*backs[c][:4])

    loads[4].wait()
    result = mixed[...]
    for c in range(chunks):
        arrive(*backs[c])
        back = unpack(order_v[2], came2[c])
        result = result + jnp.dot(
            back, wo[2 * c * LANES : 2 * (c + 1) * LANES, :], preferred_element_type=jnp.float32
        )
    out[...] = result.astype(jnp.bfloat16)


def local(lats, lons, expanded, stream, land, polar, land_shift, dw_kernel, w_proj, w_qkv, w_out, rel_bias):
    rows, cols, width_exp = expanded.shape
    width = stream.shape[2]
    heads = rel_bias.shape[0]
    count = rows * cols
    team = lats * GRID
    assert rows * lats == GRID * lats and count == LANES and GRID * (2 * GRID - 1) <= LANES
    table = jnp.transpose(rel_bias, (1, 2, 0)).reshape(-1, heads)
    home, away = orders(rows, cols, lats)
    rim_picks, spread, rim_home, inner_home = rim_tables(rows, cols, home)
    rim_count = len(rim_picks)
    assert cols & (cols - 1) == 0 and width_exp % (6 * LANES) == 0
    bf16, f32 = jnp.bfloat16, jnp.float32
    slabs = (team, 2 * count // team, width // 2)
    chunks = width // (2 * LANES)
    pieces = (chunks, team, 2 * count // team, LANES)
    any_ = pl.BlockSpec(memory_space=pl.ANY)
    vmem = pl.BlockSpec(memory_space=pltpu.VMEM)
    dma = pltpu.SemaphoreType.DMA
    result = pl.pallas_call(
        functools.partial(kernel, lats, lons, heads),
        out_shape=pltpu.VMEM((count, width), bf16),
        in_specs=[any_] * 18,
        out_specs=vmem,
        scratch_shapes=[
            pltpu.VMEM((rows + 2, cols, width_exp), bf16),
            pltpu.VMEM((2, rows, width_exp), bf16),
            pltpu.VMEM((4, 1, width_exp), f32),
            pltpu.VMEM((2, rows, width_exp), bf16),
            pltpu.VMEM((4, 1, width_exp), f32),
            pltpu.VMEM((count, width), bf16),
            pltpu.VMEM(w_proj.shape, bf16),
            pltpu.VMEM(w_qkv.shape, bf16),
            pltpu.VMEM(w_out.shape, bf16),
            pltpu.VMEM((4, rows, width_exp), f32),
            pltpu.VMEM((2, cols, width_exp), f32),
            pltpu.VMEM((2, rows, width_exp), f32),
            pltpu.VMEM((count - 2 * cols, width_exp), bf16),
            pltpu.VMEM((rim_count, width_exp), bf16),
            pltpu.VMEM((rim_count, width), f32),
            pltpu.VMEM((2 * count, width // 2), f32),
            pltpu.VMEM(slabs, bf16),
            pltpu.VMEM((rows, cols, LANES), f32),
            pltpu.VMEM((LANES, LANES), f32),
            pltpu.VMEM((count, width), f32),
            pltpu.VMEM((heads, GRID, LANES), f32),
            pltpu.VMEM((heads, GRID * GRID, LANES), f32),
            pltpu.VMEM((count, 3 * width), bf16),
            pltpu.VMEM(slabs, bf16),
            pltpu.VMEM(slabs, bf16),
            pltpu.VMEM(pieces, bf16),
            pltpu.VMEM(pieces, bf16),
            pltpu.VMEM((3,) + home.shape, bf16),
            pltpu.VMEM(inner_home.shape, bf16),
            pltpu.VMEM(rim_home.shape, bf16),
            pltpu.VMEM(rim_picks.shape, bf16),
            pltpu.VMEM(spread.shape, bf16),
            pltpu.SMEM(polar.shape, jnp.int32),
            pltpu.VMEM(land.shape, jnp.int32),
            pltpu.VMEM((1, width_exp), f32),
            pltpu.VMEM(dw_kernel.shape, f32),
            pltpu.VMEM(table.shape, f32),
            pltpu.VMEM((10 * 8, count), bf16),
            dma((18,)),
            dma((8,)),
            dma((8,)),
            dma,
            dma,
            dma((chunks,)),
            dma((chunks,)),
            dma((1 + chunks,)),
        ],
        compiler_params=pltpu.CompilerParams(collective_id=0, has_side_effects=True),
        name="section",
    )(
        expanded,
        stream.reshape(count, width),
        w_proj,
        w_qkv,
        w_out,
        polar,
        land,
        land_shift[None],
        dw_kernel,
        table,
        jnp.asarray(edge_picks(rows, cols), bf16),
        jnp.asarray(inner_home, bf16),
        jnp.asarray(rim_home, bf16),
        jnp.asarray(home.T, bf16),
        jnp.asarray(away, bf16),
        jnp.asarray(away.T, bf16),
        jnp.asarray(rim_picks, bf16),
        jnp.asarray(spread, bf16),
    )
    return result.reshape(rows, cols, width)


def solution(mesh):
    in_specs = (P("lat", "lon", None),) * 2 + (P("lat", "lon"),) + (P(),) * 7
    out_specs = P("lat", "lon", None)
    body = functools.partial(local, mesh.shape["lat"], mesh.shape["lon"])
    return jax.shard_map(body, mesh=mesh, in_specs=in_specs, out_specs=out_specs, check_vma=False)
```
